128 devices in a mesh: dp: 4 (over x), space: 32 (over y, z, core).
Axes of the slice: x: 4, y: 4, z: 4, core: 2. Of those that a mesh axis runs over, the one named last changes fastest.
Arguments:
- fields: bfloat16 [4, 256, 64, 4096], P('dp', 'space'), may hold values from -6 to 6
- cotangent: bfloat16 [4, 256, 64, 4096], P('dp', 'space'), may hold values from -6 to 6
- mode_weight: bfloat16 [128, 64, 64, 128], P('space'), may hold values from -4 to 4
- mix_weight: bfloat16 [64, 64], replicated, may hold values from -0.75 to 0.75
Outputs:
- response: bfloat16 [4, 256, 64, 4096], P('dp', 'space')
- field_grad: bfloat16 [4, 256, 64, 4096], P('dp', 'space')
- mode_grad: float32 [128, 64, 64, 128], P('space', 'dp')
The draws below stay inside these ranges and needn't reach their ends.
All inputs are finite; a program needn't handle non-finite values.
Results may differ from the reference program's by a relative error of at most 0.035.
Values may be sent and summed in bfloat16 or wider, within the bound.
No kernel may reach another device: no remote copies, remote signals or barrier semaphores. Data moves between devices by JAX's collectives and lax.ppermute only.
A program may use at most 128 MiB of HBM per device.

```python
import math
import jax
import jax.numpy as jnp
from jax import lax

C = 64
KX = 64
KY = 128
NY = 4096
NX = 256
SAMPLES = 4


def block_scale(stream_key, dims, cuts, smallest, top_value):
    loudness = 1.0
    for axis_at, parts in cuts:
        draws = jax.random.uniform(jax.random.fold_in(jax.random.fold_in(stream_key, 6), axis_at), (parts,), jnp.float32, smallest / len(cuts), top_value / len(cuts))
        loudness = loudness * jnp.repeat(jnp.exp(draws), dims[axis_at] // parts).reshape((-1,) + (1,) * (len(dims) - 1 - axis_at))
    return loudness


def bell_draw(own_key, shape, scale, bound, pieces=(), held_as=jnp.bfloat16):
    level = block_scale(own_key, shape, pieces, -0.22, 0.18) if pieces else 1.0
    values = jax.random.normal(own_key, shape, jnp.float32) * scale * level
    return jnp.minimum(jnp.maximum(values, -bound), bound).astype(held_as)


def setup_inputs(seed: int = 0) -> dict:
    keys = jax.random.split(jax.random.key(seed), 5)
    fields = bell_draw(keys[0], (SAMPLES, NX, C, NY), 1.0, 6.0, ((0, 4), (1, 32)))
    cotangent = bell_draw(keys[1], (SAMPLES, NX, C, NY), 1.0, 6.0, ((0, 4), (1, 32)))
    mode_weight = bell_draw(keys[2], (KY, KX, C, 2 * C), (max(1, 4 * KX * KY * C // (NX * NY))) ** -0.5, 4.0, ((0, 32),))
    mix_weight = bell_draw(keys[3], (C, C), C ** -0.5, 0.75)
    return {"fields": fields, "cotangent": cotangent, "mode_weight": mode_weight, "mix_weight": mix_weight}


GELU_CUBIC = 0.044715
GELU_SCALE = math.sqrt(2.0 / math.pi)

def gelu_value(values):
    inner_arg = GELU_SCALE * (values + GELU_CUBIC * values * values * values)
    return 0.5 * values * (1.0 + jnp.tanh(inner_arg))

def gelu_slope(values):
    tangent = jnp.tanh(GELU_SCALE * (values + GELU_CUBIC * values * values * values))
    return 0.5 * (1.0 + tangent) + 0.5 * values * (1.0 - tangent * tangent) * GELU_SCALE * (1.0 + 3.0 * GELU_CUBIC * values * values)

def column_angles(length, mode_count):
    positions = lax.iota(jnp.int32, length)
    frequencies = lax.iota(jnp.int32, mode_count)
    phase_index = positions[:, None] * frequencies[None, :] % length
    return phase_index.astype(jnp.float32) * (2.0 * math.pi / length)

def column_factor(mode_count):
    frequencies = lax.iota(jnp.int32, mode_count)
    single = jnp.where(frequencies == 0, 1.0, 2.0).astype(jnp.bfloat16)
    return jnp.concatenate([single, single], axis=0)

def forward_table(length, mode_count, weighted):
    angles = column_angles(length, mode_count)
    norm_scale = 1.0 / math.sqrt(length)
    table_out = jnp.concatenate([jnp.cos(angles) * norm_scale, -jnp.sin(angles) * norm_scale], axis=1).astype(jnp.bfloat16)
    if weighted:
        table_out = table_out * column_factor(mode_count)[None, :]
    return table_out

def inverse_table(length, mode_count, weighted):
    angles = column_angles(length, mode_count).T
    norm_scale = 1.0 / math.sqrt(length)
    table_out = jnp.concatenate([jnp.cos(angles) * norm_scale, -jnp.sin(angles) * norm_scale], axis=0).astype(jnp.bfloat16)
    if weighted:
        table_out = table_out * column_factor(mode_count)[:, None]
    return table_out

def row_tables(extent, mode_count, offset, length):
    slot_index = lax.iota(jnp.int32, mode_count)
    frequencies = jnp.where(slot_index < mode_count // 2, slot_index, extent - mode_count + slot_index)
    rows_here = offset + lax.iota(jnp.int32, length)
    phase_index = frequencies[:, None] * rows_here[None, :] % extent
    angles = phase_index.astype(jnp.float32) * (2.0 * math.pi / extent)
    norm_scale = 1.0 / math.sqrt(extent)
    return ((jnp.cos(angles) * norm_scale).astype(jnp.bfloat16), (jnp.sin(angles) * norm_scale).astype(jnp.bfloat16))

def row_forward(cos_table, sin_table, columns):
    cos_part = jnp.einsum('kr,rcpy->ykpc', cos_table.astype(jnp.float32), columns.astype(jnp.float32))
    sin_part = jnp.einsum('kr,rcpy->ykpc', sin_table.astype(jnp.float32), columns.astype(jnp.float32))
    real_part = cos_part[:, :, 0] + sin_part[:, :, 1]
    imag_part = cos_part[:, :, 1] - sin_part[:, :, 0]
    return jnp.concatenate([real_part, imag_part], axis=-1)

def row_inverse(cos_table, sin_table, spectrum):
    channels = spectrum.shape[2] // 2
    cos_part = jnp.einsum('kr,ykd->rdy', cos_table.astype(jnp.float32), spectrum.astype(jnp.float32))
    sin_part = jnp.einsum('kr,ykd->rdy', sin_table.astype(jnp.float32), spectrum.astype(jnp.float32))
    real_part = cos_part[:, :channels] - sin_part[:, channels:]
    imag_part = cos_part[:, channels:] + sin_part[:, :channels]
    return jnp.stack([real_part, imag_part], axis=2)

def mix_modes(spectrum, weight):
    channels = weight.shape[2]
    real_prod = jnp.einsum('ykc,ykcd->ykd', spectrum[..., :channels].astype(jnp.float32), weight.astype(jnp.float32))
    imag_prod = jnp.einsum('ykc,ykcd->ykd', spectrum[..., channels:].astype(jnp.float32), weight.astype(jnp.float32))
    return jnp.concatenate([real_prod[..., :channels] - imag_prod[..., channels:], real_prod[..., channels:] + imag_prod[..., :channels]], axis=-1)

def mix_adjoint(delta_modes, weight):
    channels = weight.shape[2]
    swapped = jnp.concatenate([delta_modes[..., channels:], -delta_modes[..., :channels]], axis=-1)
    first_half = jnp.einsum('ykd,ykcd->ykc', delta_modes.astype(jnp.float32), weight.astype(jnp.float32))
    second_half = jnp.einsum('ykd,ykcd->ykc', swapped.astype(jnp.float32), weight.astype(jnp.float32))
    return jnp.concatenate([first_half, second_half], axis=-1)

def weight_grad(spectrum, delta_modes):
    channels = spectrum.shape[2] // 2
    swapped = jnp.concatenate([delta_modes[..., channels:], -delta_modes[..., :channels]], axis=-1)
    real_term = jnp.einsum('ykc,ykd->ykcd', spectrum[..., :channels].astype(jnp.float32), delta_modes.astype(jnp.float32))
    imag_term = jnp.einsum('ykc,ykd->ykcd', spectrum[..., channels:].astype(jnp.float32), swapped.astype(jnp.float32))
    return real_term + imag_term

def reference(fields, cotangent, mode_weight, mix_weight):
    forward_cols = forward_table(NY, KY, False)
    weighted_cols = forward_table(NY, KY, True)
    inverse_cols = inverse_table(NY, KY, True)
    plain_inverse = inverse_table(NY, KY, False)
    whole_cos, whole_sin = row_tables(NX, KX, 0, NX)
    mixer = mix_weight.astype(jnp.float32)

    def one_sample(running, sample_pair):
        signal, upstream = sample_pair
        columns = jnp.dot(signal.reshape(NX * C, NY), forward_cols, preferred_element_type=jnp.float32)
        columns = columns.astype(jnp.bfloat16).reshape(NX, C, 2, KY)
        spectrum = row_forward(whole_cos, whole_sin, columns).astype(jnp.bfloat16)
        modes_out = mix_modes(spectrum, mode_weight).astype(jnp.bfloat16)
        back_columns = row_inverse(whole_cos, whole_sin, modes_out).astype(jnp.bfloat16)
        spectral = jnp.dot(back_columns.reshape(NX * C, 2 * KY), inverse_cols, preferred_element_type=jnp.float32).reshape(NX, C, NY)
        preact = spectral + jnp.einsum('rcn,cd->rdn', signal.astype(jnp.float32), mixer)
        response = gelu_value(preact).astype(jnp.bfloat16)
        delta_field = (upstream.astype(jnp.float32) * gelu_slope(preact)).astype(jnp.bfloat16)
        delta_cols = jnp.dot(delta_field.reshape(NX * C, NY), weighted_cols, preferred_element_type=jnp.float32)
        delta_cols = delta_cols.astype(jnp.bfloat16).reshape(NX, C, 2, KY)
        delta_modes = row_forward(whole_cos, whole_sin, delta_cols).astype(jnp.bfloat16)
        input_modes = mix_adjoint(delta_modes, mode_weight).astype(jnp.bfloat16)
        grad_here = weight_grad(spectrum, delta_modes)
        input_cols = row_inverse(whole_cos, whole_sin, input_modes).astype(jnp.bfloat16)
        field_grad = jnp.dot(input_cols.reshape(NX * C, 2 * KY), plain_inverse, preferred_element_type=jnp.float32).reshape(NX, C, NY)
        field_grad = field_grad + jnp.einsum('rdn,cd->rcn', delta_field.astype(jnp.float32), mixer)
        return (running + grad_here, (response, field_grad.astype(jnp.bfloat16)))
    start_grad = jnp.zeros((KY, KX, C, 2 * C), jnp.float32)
    grad_total, outputs = lax.scan(one_sample, start_grad, (fields, cotangent))
    return (outputs[0], outputs[1], grad_total)
```

```python
import math

import jax
import jax.numpy as jnp
import numpy as np
from jax import lax
from jax.sharding import PartitionSpec as P

GELU_CUBIC = 0.044715
GELU_SCALE = math.sqrt(2.0 / math.pi)


def gelu_value(values):
    inner_arg = GELU_SCALE * (values + GELU_CUBIC * values * values * values)
    return 0.5 * values * (1.0 + jnp.tanh(inner_arg))


def gelu_slope(values):
    tangent = jnp.tanh(GELU_SCALE * (values + GELU_CUBIC * values * values * values))
    return 0.5 * (1.0 + tangent) + 0.5 * values * (1.0 - tangent * tangent) * GELU_SCALE * (
        1.0 + 3.0 * GELU_CUBIC * values * values
    )


def trig(phase_index, period, extent):
    angles = phase_index.astype(np.float32) * np.float32(2.0 * math.pi / period)
    norm_scale = np.float32(1.0 / math.sqrt(extent))
    rounded = jnp.bfloat16
    return (
        (np.cos(angles) * norm_scale).astype(rounded),
        (np.sin(angles) * norm_scale).astype(rounded),
    )


def column_table(length, mode_count, owners):
    phase = np.arange(length)[:, None] * np.arange(mode_count)[None, :] % length
    cos_part, sin_part = trig(phase, length, length)
    both = np.stack([cos_part, -sin_part], axis=1)
    both = both.reshape(length, 2, owners, mode_count // owners)
    return both.transpose(0, 2, 1, 3).reshape(length, 2 * mode_count)


def column_weight(mode_count, owners):
    single = np.where(np.arange(mode_count) == 0, 1.0, 2.0).astype(np.float32)
    both = np.stack([single, single]).reshape(2, owners, mode_count // owners)
    return both.transpose(1, 0, 2).reshape(2 * mode_count)


def row_tables(extent, mode_count):
    slot = np.arange(mode_count)
    frequency = np.where(slot < mode_count // 2, slot, extent - mode_count + slot)
    phase = frequency[:, None] * np.arange(extent)[None, :] % extent
    return trig(phase, extent, extent)


def mix_modes(spectrum, weight):
    channels = weight.shape[2]
    real_prod = jnp.einsum(
        "ykc,ykcd->ykd", spectrum[..., :channels], weight, preferred_element_type=jnp.float32
    )
    imag_prod = jnp.einsum(
        "ykc,ykcd->ykd", spectrum[..., channels:], weight, preferred_element_type=jnp.float32
    )
    return jnp.concatenate(
        [
            real_prod[..., :channels] - imag_prod[..., channels:],
            real_prod[..., channels:] + imag_prod[..., :channels],
        ],
        axis=-1,
    )


def mix_adjoint(delta_modes, weight):
    channels = weight.shape[2]
    swapped = jnp.concatenate([delta_modes[..., channels:], -delta_modes[..., :channels]], axis=-1)
    first_half = jnp.einsum(
        "ykd,ykcd->ykc", delta_modes, weight, preferred_element_type=jnp.float32
    )
    second_half = jnp.einsum("ykd,ykcd->ykc", swapped, weight, preferred_element_type=jnp.float32)
    return jnp.concatenate([first_half, second_half], axis=-1)


def on_device(fields, cotangent, mode_weight, mix_weight):
    signal = fields[0]
    upstream = cotangent[0]
    rows_here, channels, length = signal.shape
    mode_rows, kx_count = mode_weight.shape[:2]
    groups = lax.axis_size("space")
    ky_count = mode_rows * groups
    extent = rows_here * groups
    table = jnp.asarray(column_table(length, ky_count, groups))
    weight = jnp.asarray(column_weight(ky_count, groups))
    row_cos, row_sin = row_tables(extent, kx_count)
    forward_rows = jnp.asarray(
        np.block([[row_cos, row_sin], [-row_sin, row_cos]]).reshape(
            2, kx_count, 2, groups, rows_here
        )
    )

    def exchange(values, axis):
        return lax.all_to_all(values, axis, 0, 0, tiled=True)

    def to_modes(columns):
        sent = columns.astype(jnp.bfloat16).reshape(groups, 2 * mode_rows, rows_here * channels)
        got = exchange(sent, "space").reshape(groups, 2, mode_rows, rows_here, channels)
        modes = jnp.einsum(
            "qjpsr,spirc->ijqc", forward_rows, got, preferred_element_type=jnp.float32
        )
        return modes.astype(jnp.bfloat16).reshape(mode_rows, kx_count, 2 * channels)

    def to_rows(modes):
        parts = modes.reshape(mode_rows, kx_count, 2, channels)
        back = jnp.einsum(
            "qjpsr,ijqc->spirc", forward_rows, parts, preferred_element_type=jnp.float32
        ).astype(jnp.bfloat16)
        sent = back.reshape(groups, 2 * mode_rows, rows_here * channels)
        return exchange(sent, "space").reshape(2 * ky_count, rows_here * channels)

    def by_kx(modes):
        samples = lax.axis_size("dp")
        parts = modes.reshape(mode_rows, samples, kx_count // samples, 2 * channels)
        return exchange(parts.transpose(1, 0, 2, 3), "dp")

    flat_signal = signal.reshape(rows_here * channels, length)
    columns = jnp.einsum("nm,xn->mx", table, flat_signal, preferred_element_type=jnp.float32)
    spectrum = to_modes(columns)
    modes_out = mix_modes(spectrum, mode_weight).astype(jnp.bfloat16)
    back_columns = to_rows(modes_out)
    spectral = jnp.einsum(
        "mx,nm->xn",
        back_columns * weight[:, None].astype(jnp.bfloat16),
        table,
        preferred_element_type=jnp.float32,
    ).reshape(rows_here, channels, length)
    preact = spectral + jnp.einsum(
        "rcn,cd->rdn", signal, mix_weight, preferred_element_type=jnp.float32
    )
    response = gelu_value(preact).astype(jnp.bfloat16)
    delta_field = (upstream.astype(jnp.float32) * gelu_slope(preact)).astype(jnp.bfloat16)
    delta_cols = (
        jnp.einsum(
            "nm,xn->mx",
            table,
            delta_field.reshape(rows_here * channels, length),
            preferred_element_type=jnp.float32,
        )
        * weight[:, None]
    )
    delta_modes = to_modes(delta_cols)
    input_modes = mix_adjoint(delta_modes, mode_weight).astype(jnp.bfloat16)
    input_cols = to_rows(input_modes)
    all_x = by_kx(spectrum)
    all_dy = by_kx(delta_modes)
    swapped = jnp.concatenate([all_dy[..., channels:], -all_dy[..., :channels]], axis=-1)
    mode_grad = jnp.einsum(
        "sykc,sykd->ykcd", all_x[..., :channels], all_dy, preferred_element_type=jnp.float32
    ) + jnp.einsum(
        "sykc,sykd->ykcd", all_x[..., channels:], swapped, preferred_element_type=jnp.float32
    )
    field_grad = jnp.einsum(
        "mx,nm->xn", input_cols, table, preferred_element_type=jnp.float32
    ).reshape(rows_here, channels, length)
    field_grad = field_grad + jnp.einsum(
        "rdn,cd->rcn", delta_field, mix_weight, preferred_element_type=jnp.float32
    )
    return (response[None], field_grad.astype(jnp.bfloat16)[None], mode_grad)


def solution(mesh):
    in_specs = (
        P("dp", "space", None, None),
        P("dp", "space", None, None),
        P("space", None, None, None),
        P(),
    )
    out_specs = (
        P("dp", "space", None, None),
        P("dp", "space", None, None),
        P("space", "dp", None, None),
    )
    return jax.shard_map(
        on_device, mesh=mesh, in_specs=in_specs, out_specs=out_specs, check_vma=False
    )
```

```python
import math

import jax
import jax.numpy as jnp
import numpy as np
from jax import lax
from jax.experimental import pallas as pl
from jax.experimental.pallas import tpu as pltpu
from jax.sharding import PartitionSpec as P

GELU_CUBIC = 0.044715
GELU_SCALE = math.sqrt(2.0 / math.pi)
LANES = 128
BF16 = jnp.bfloat16
F32 = jnp.float32
STACK = 4
TILE = 512
DIAGONAL = 256
AHEAD = 3
MIB = 1024 * 1024


def trig(phase_index, extent):
    angles = phase_index.astype(np.float32) * np.float32(2.0 * math.pi / extent)
    norm_scale = np.float32(1.0 / math.sqrt(extent))
    return (
        (np.cos(angles) * norm_scale).astype(BF16).astype(np.float32),
        (np.sin(angles) * norm_scale).astype(BF16).astype(np.float32),
    )


def column_table(length, mode_count, owners):
    phase = np.arange(mode_count)[:, None] * np.arange(length)[None, :] % length
    cos_part, sin_part = trig(phase, length)
    both = np.stack([cos_part, -sin_part]).reshape(2, owners, mode_count // owners, length)
    return both.transpose(1, 0, 2, 3).reshape(2 * mode_count, length).astype(BF16)


def row_matrix(extent, mode_count):
    slot = np.arange(mode_count)
    frequency = np.where(slot < mode_count // 2, slot, extent - mode_count + slot)
    phase = frequency[:, None] * np.arange(extent)[None, :] % extent
    cos_part, sin_part = trig(phase, extent)
    return np.stack(
        [np.stack([cos_part, sin_part], 1), np.stack([-sin_part, cos_part], 1)], 1
    )


def split_rows(matrix, owners):
    rows, parts, extent = matrix.shape
    split = matrix.reshape(rows, parts, owners, extent // owners // 2, 2)
    split = split.transpose(4, 0, 1, 3, 2)
    return split.reshape(2, rows, parts * extent // 2)


def half_mask(shape):
    return lax.broadcasted_iota(jnp.int32, shape, len(shape) - 1) % LANES < LANES // 2


def fold(first, second):
    picked = jnp.where(half_mask(first.shape), first, second)
    return picked + pltpu.roll(picked, LANES // 2, 1)


def dot_nt(left, right):
    return lax.dot_general(left, right, (((1,), (1,)), ((), ())), preferred_element_type=F32)


def dot_nn(left, right):
    return jnp.dot(left, right, preferred_element_type=F32)


def weigh(values, mode_rows):
    row = lax.broadcasted_iota(jnp.int32, values.shape, 0)
    return jnp.where((row == 0) | (row == mode_rows), values, values * 2.0)


def tiles(length):
    return [slice(at, at + TILE) for at in range(0, length, TILE)]


class Loads:
    def __init__(self, pairs, sem_ref, ahead):
        self.copies = [
            [
                pltpu.make_async_copy(source.at[:, cols], target.at[:, cols], sem_ref.at[n, k])
                for n, (source, target) in enumerate(pairs)
            ]
            for k, cols in enumerate(tiles(pairs[0][0].shape[1]))
        ]
        self.ahead = ahead
        for k in range(ahead):
            self.start(k)

    def start(self, k):
        if k < len(self.copies):
            for copy in self.copies[k]:
                copy.start()

    def wait(self, k):
        for copy in self.copies[k]:
            copy.wait()
        self.start(k + self.ahead)


def columns_kernel(table_hbm, fields_hbm, out_ref, fields_ref, table_ref, acc_ref, sem_ref):
    parts = tiles(table_hbm.shape[1])
    loads = Loads(((table_hbm, table_ref), (fields_hbm, fields_ref)), sem_ref, AHEAD)
    for k, cols in enumerate(parts):
        loads.wait(k)
        product = dot_nt(table_ref[:, cols], fields_ref[:, cols])
        if k == 0:
            acc_ref[...] = product
        elif k < len(parts) - 1:
            acc_ref[...] += product
        else:
            out_ref[...] = (acc_ref[...] + product).reshape(out_ref.shape).astype(BF16)


def gather_rows(got_ref, flat_ref, z_ref):
    owners, slots, width = got_ref.shape
    mode_rows = slots // 2
    for h in range(width // LANES):
        part = got_ref[:, :, h * LANES : (h + 1) * LANES].astype(F32)
        flat_ref[h] = part.reshape(owners * slots, LANES)
    for p in range(2):
        for i in range(mode_rows):
            for h in range(width // LANES):
                block = flat_ref[h, pl.ds(p * mode_rows + i, owners, stride=slots), :]
                at = (p * (width // LANES) + h) * owners
                z_ref[i, at : at + owners, :] = block.astype(BF16)


def scatter_rows(values, flat_ref, i, owners, slots):
    mode_rows = slots // 2
    columns = flat_ref.shape[0]
    for p in range(2):
        for h in range(columns):
            at = (p * columns + h) * owners
            flat_ref[h, pl.ds(p * mode_rows + i, owners, stride=slots), :] = values[
                at : at + owners
            ]


def modes_kernel(
    place_ref, got_ref, weight_ref, rows_ref, back_ref, *rest, adjoint, samples
):
    given = samples if adjoint else 0
    x_refs, sent_ref, shared_refs = rest[:given], rest[given], rest[given + 1 : given + 1 + samples]
    flat_ref, z_ref, mode_ref, y_ref = rest[given + 1 + samples :]
    owners, slots, _ = got_ref.shape
    mode_rows, kx_count, channels, _ = weight_ref.shape
    gather_rows(got_ref, flat_ref, z_ref)
    count = 2 * kx_count
    stack_rows = 2 * STACK
    for i in range(mode_rows):
        z = z_ref[i]
        both = fold(dot_nn(rows_ref[0], z), dot_nn(rows_ref[1], z))
        if adjoint:
            plain, turned = both[:count], both[count:]
            left = jnp.where(half_mask(plain.shape), plain, turned)
            mode_ref[i] = left
            left = left.astype(BF16)
            row = lax.broadcasted_iota(jnp.int32, (stack_rows, LANES), 0) // 2
            low = half_mask((stack_rows, LANES))
            for g in range(kx_count // STACK):
                pair = left[g // 2 * 2 * stack_rows : (g // 2 + 1) * 2 * stack_rows]
                w = weight_ref[i, g * STACK : (g + 1) * STACK].reshape(STACK * channels, LANES)
                full = dot_nt(pair, w)[g % 2 * stack_rows : (g % 2 + 1) * stack_rows]
                picked = jnp.where(row < 2, full[:, :LANES], full[:, LANES:])
                picked = jnp.where((row % 2 == 0) == low, picked, 0.0)
                y_ref[g * stack_rows : (g + 1) * stack_rows, :] = picked + pltpu.roll(
                    picked, LANES // 2, 1
                )
        else:
            wide = jnp.concatenate([both, both], axis=1)
            lane = lax.broadcasted_iota(jnp.int32, wide.shape, 1) // channels
            row = lax.broadcasted_iota(jnp.int32, wide.shape, 0) % stack_rows // 2
            left = jnp.where(lane == row, wide, 0.0).astype(BF16)
            for g in range(kx_count // STACK):
                rows = slice(g * 2 * stack_rows, (g + 1) * 2 * stack_rows)
                mode_ref[i, g * stack_rows : (g + 1) * stack_rows, :] = both[rows][:stack_rows]
                w = weight_ref[i, g * STACK : (g + 1) * STACK].reshape(STACK * channels, LANES)
                full = dot_nn(left[rows], w)
                y_ref[g * stack_rows : (g + 1) * stack_rows, :] = fold(
                    full[:stack_rows], full[stack_rows:]
                )
        y = y_ref[...].astype(BF16)
        low = half_mask((back_ref.shape[1], LANES))
        values = jnp.where(low, dot_nn(back_ref[0], y), dot_nn(back_ref[1], y))
        scatter_rows(values, flat_ref, i, owners, slots)
    for h in range(flat_ref.shape[0]):
        part = flat_ref[h].reshape(owners, slots, LANES)
        sent_ref[:, :, h * LANES : (h + 1) * LANES] = part.astype(BF16)
    block = count // samples
    for k, shared_ref in enumerate(shared_refs):
        start = pl.multiple_of((place_ref[0] + k) % samples * block, block)
        if adjoint:
            shared_ref[0] = x_refs[k][...]
        for i in range(mode_rows):
            values = mode_ref[i, pl.ds(start, block), :].astype(BF16)
            if adjoint:
                shared_ref[1, i] = values
            else:
                shared_ref[i] = values


def transposed_back(back_ref, mode_rows, weighted):
    owners, slots, width = back_ref.shape
    flat = back_ref[...].astype(F32).reshape(owners * slots, width)
    if weighted:
        flat = weigh(flat, mode_rows)
    return flat.T.astype(BF16)


def spread(block, out_ref):
    out_ref[...] = jnp.zeros_like(out_ref)
    size = block.shape[0]
    for at in range(0, out_ref.shape[0], size):
        out_ref[at : at + size, at : at + size] = block


def field_kernel(
    back_ref, table_ref, fields_ref, upstream_hbm, weight_ref,
    response_hbm, delta_hbm, sent_ref,
    upstream_ref, response_ref, delta_ref, turned_ref, mix_ref, pre_ref, acc_ref, sem_ref,
):
    loads = Loads(((upstream_hbm, upstream_ref),), sem_ref, AHEAD)
    mode_rows = back_ref.shape[1] // 2
    turned_ref[...] = transposed_back(back_ref, mode_rows, True)
    spread(weight_ref[...].astype(F32).T.astype(BF16), mix_ref)
    width = mix_ref.shape[0]
    total = fields_ref.shape[0]
    chunk = 32
    parts = tiles(table_ref.shape[1])
    copies = []
    for k, cols in enumerate(parts):
        slot = k % pre_ref.shape[0]
        for at in range(0, total, width):
            rows = slice(at, at + width)
            pre_ref[slot, rows, :] = dot_nn(turned_ref[rows, :], table_ref[:, cols]) + dot_nn(
                mix_ref[...], fields_ref[rows, cols]
            )
        loads.wait(k)
        for at in range(0, total, chunk):
            rows = slice(at, at + chunk)
            v = pre_ref[slot, rows, :]
            square = v * v
            half = 0.5 + 0.5 * jnp.tanh(v * (GELU_SCALE + (GELU_SCALE * GELU_CUBIC) * square))
            value = v * half
            response_ref[rows, cols] = value.astype(BF16)
            slope = half + value * (1.0 - half) * (
                2.0 * GELU_SCALE + (6.0 * GELU_SCALE * GELU_CUBIC) * square
            )
            delta_ref[rows, cols] = (upstream_ref[rows, cols].astype(F32) * slope).astype(BF16)
        for n, (source, target) in enumerate(
            ((response_ref, response_hbm), (delta_ref, delta_hbm))
        ):
            copies.append(
                pltpu.make_async_copy(
                    source.at[:, cols], target.at[:, cols], sem_ref.at[1 + n, k]
                )
            )
            copies[-1].start()
        product = dot_nt(table_ref[:, cols], delta_ref[:, cols])
        if k == 0:
            acc_ref[...] = product
        elif k < len(parts) - 1:
            acc_ref[...] += product
        else:
            sent = weigh(acc_ref[...] + product, mode_rows)
            sent_ref[...] = sent.reshape(sent_ref.shape).astype(BF16)
    for copy in copies:
        copy.wait()


def grad_kernel(
    back_ref, table_ref, delta_hbm, weight_ref, out_hbm,
    delta_ref, turned_ref, mix_ref, out_ref, sem_ref,
):
    loads = Loads(((delta_hbm, delta_ref),), sem_ref, AHEAD)
    turned_ref[...] = transposed_back(back_ref, 0, False)
    spread(weight_ref[...], mix_ref)
    width = mix_ref.shape[0]
    copies = []
    for k, cols in enumerate(tiles(table_ref.shape[1])):
        loads.wait(k)
        for at in range(0, delta_ref.shape[0], width):
            rows = slice(at, at + width)
            out_ref[rows, cols] = (
                dot_nn(turned_ref[rows, :], table_ref[:, cols])
                + dot_nn(mix_ref[...], delta_ref[rows, cols])
            ).astype(BF16)
        copy = pltpu.make_async_copy(out_ref.at[:, cols], out_hbm.at[:, cols], sem_ref.at[1, k])
        copy.start()
        copies.append(copy)
    for copy in copies:
        copy.wait()


def mode_grad_kernel(*refs, samples):
    shared_refs, out_ref = refs[:samples], refs[samples]
    mode_rows, kx_here, channels, _ = out_ref.shape
    stack_rows = 2 * STACK
    count = samples * stack_rows
    row = lax.broadcasted_iota(jnp.int32, (count, LANES), 0) % stack_rows // 2
    for i in range(mode_rows):
        for g in range(kx_here // STACK):
            rows = slice(g * stack_rows, (g + 1) * stack_rows)
            x = jnp.concatenate([ref[0, i, rows, :].astype(F32) for ref in shared_refs], axis=0)
            d = jnp.concatenate([ref[1, i, rows, :].astype(F32) for ref in shared_refs], axis=0)
            wide = jnp.concatenate(
                [jnp.where(row == m, d, 0.0) for m in range(STACK)], axis=1
            ).astype(BF16)
            turned = x.T[:channels].astype(BF16)
            product = dot_nn(turned, wide)
            for m in range(STACK):
                out_ref[i, g * STACK + m] = product[:, m * LANES : (m + 1) * LANES]


VMEM = pl.BlockSpec(memory_space=pltpu.VMEM)
HBM = pl.BlockSpec(memory_space=pltpu.HBM)


def pinned(values):
    return pltpu.with_memory_space_constraint(values, pltpu.HBM)


def params(mib):
    return pltpu.CompilerParams(vmem_limit_bytes=mib * MIB)


def on_device(fields, cotangent, mode_weight, mix_weight):
    _, rows_here, channels, length = fields.shape
    mode_rows, kx_count = mode_weight.shape[:2]
    groups = lax.axis_size("space")
    samples = lax.axis_size("dp")
    ky_count = mode_rows * groups
    extent = rows_here * groups
    lines = rows_here * channels
    slots = 2 * mode_rows
    signal = fields.reshape(lines, length)
    upstream = cotangent.reshape(lines, length)
    table = jnp.asarray(column_table(length, ky_count, groups))
    matrix = row_matrix(extent, kx_count)
    turned = np.stack([-matrix[:, 1], matrix[:, 0]], 1)
    plain_rows = matrix.reshape(2 * kx_count, 2, extent)
    turned_rows = turned.reshape(2 * kx_count, 2, extent)
    grouped = np.concatenate(
        [
            part.reshape(kx_count // STACK, 2 * STACK, 2, extent)
            for part in (plain_rows, turned_rows)
        ],
        axis=1,
    ).reshape(4 * kx_count, 2, extent)
    mix_rows = jnp.asarray(split_rows(grouped, groups).astype(BF16))
    adjoint_rows = jnp.asarray(
        split_rows(np.concatenate([plain_rows, -turned_rows]), groups).astype(BF16)
    )
    back_rows = jnp.asarray(
        split_rows(plain_rows, groups).transpose(0, 2, 1).astype(BF16)
    )
    place = lax.axis_index("dp").astype(jnp.int32).reshape(1)

    exchange_shape = jax.ShapeDtypeStruct((groups, slots, lines), BF16)
    lines_shape = pltpu.HBM((lines, length), BF16)
    steps = length // TILE

    def exchange(values):
        return lax.all_to_all(values, "space", 0, 0, tiled=True)

    def mix(got, rows, given):
        adjoint = bool(given)
        shape = (mode_rows, 2 * kx_count // samples, LANES)
        block = jax.ShapeDtypeStruct((2,) + shape if adjoint else shape, BF16)
        outs = pl.pallas_call(
            lambda *refs: modes_kernel(*refs, adjoint=adjoint, samples=samples),
            out_shape=[exchange_shape] + [block] * samples,
            in_specs=[pl.BlockSpec(memory_space=pltpu.SMEM)] + [VMEM] * (4 + len(given)),
            out_specs=[VMEM] * (1 + samples),
            scratch_shapes=[
                pltpu.VMEM((lines // LANES, groups * slots, LANES), F32),
                pltpu.VMEM((mode_rows, rows_here * groups, LANES), BF16),
                pltpu.VMEM((mode_rows, 2 * kx_count, LANES), F32),
                pltpu.VMEM((2 * kx_count, LANES), F32),
            ],
            compiler_params=params(10),
            name="adjoint_modes" if adjoint else "mix_modes",
        )(place, got, mode_weight, rows, back_rows, *given)
        return outs[0], outs[1:]

    def share(blocks):
        return [blocks[0]] + [
            lax.ppermute(
                blocks[k], "dp", [(a, (a + k) % samples) for a in range(samples)]
            )
            for k in range(1, samples)
        ]

    columns, near_signal = pl.pallas_call(
        columns_kernel,
        out_shape=[exchange_shape, jax.ShapeDtypeStruct((lines, length), BF16)],
        in_specs=[HBM, HBM],
        out_specs=[VMEM, VMEM],
        scratch_shapes=[
            pltpu.VMEM(table.shape, BF16),
            pltpu.VMEM((2 * ky_count, lines), F32),
            pltpu.SemaphoreType.DMA((2, steps)),
        ],
        compiler_params=params(14),
        name="columns",
    )(pinned(table), pinned(signal))
    columns, place = lax.optimization_barrier((columns, place))
    sent, spectrum = mix(exchange(columns), mix_rows, ())
    back = exchange(sent)
    response, delta, delta_columns = pl.pallas_call(
        field_kernel,
        out_shape=[lines_shape, lines_shape, exchange_shape],
        in_specs=[VMEM, VMEM, VMEM, HBM, VMEM],
        out_specs=[HBM, HBM, VMEM],
        scratch_shapes=[pltpu.VMEM((lines, length), BF16)] * 3
        + [
            pltpu.VMEM((lines, 2 * ky_count), BF16),
            pltpu.VMEM((DIAGONAL, DIAGONAL), BF16),
            pltpu.VMEM((2, lines, TILE), F32),
            pltpu.VMEM((2 * ky_count, lines), F32),
            pltpu.SemaphoreType.DMA((3, steps)),
        ],
        compiler_params=params(20),
        name="field_step",
    )(back, table, near_signal, pinned(upstream), mix_weight)
    sent, both_modes = mix(exchange(delta_columns), adjoint_rows, spectrum)
    shared = share(both_modes)
    back = exchange(sent)
    mode_grad = pl.pallas_call(
        lambda *refs: mode_grad_kernel(*refs, samples=samples),
        out_shape=jax.ShapeDtypeStruct(
            (mode_rows, kx_count // samples, channels, LANES), F32
        ),
        in_specs=[VMEM] * samples,
        out_specs=VMEM,
        compiler_params=params(8),
        name="mode_grad",
    )(*shared)
    field_grad = pl.pallas_call(
        grad_kernel,
        out_shape=lines_shape,
        in_specs=[VMEM, VMEM, HBM, VMEM],
        out_specs=HBM,
        scratch_shapes=[
            pltpu.VMEM((lines, length), BF16),
            pltpu.VMEM((lines, 2 * ky_count), BF16),
            pltpu.VMEM((DIAGONAL, DIAGONAL), BF16),
            pltpu.VMEM((lines, length), BF16),
            pltpu.SemaphoreType.DMA((2, steps)),
        ],
        compiler_params=params(16),
        name="field_grad",
    )(back, table, pinned(delta), mix_weight)
    return (response.reshape(fields.shape), field_grad.reshape(fields.shape), mode_grad)


def solution(mesh):
    in_specs = (
        P("dp", "space", None, None),
        P("dp", "space", None, None),
        P("space", None, None, None),
        P(),
    )
    out_specs = (
        P("dp", "space", None, None),
        P("dp", "space", None, None),
        P("space", "dp", None, None),
    )
    return jax.shard_map(
        on_device, mesh=mesh, in_specs=in_specs, out_specs=out_specs, check_vma=False
    )
```

```python
import math

import jax
import jax.numpy as jnp
import numpy as np
from jax import lax
from jax.experimental import pallas as pl
from jax.experimental.pallas import tpu as pltpu
from jax.sharding import PartitionSpec as P

GELU_CUBIC = 0.044715
GELU_SCALE = math.sqrt(2.0 / math.pi)
LANES = 128
BF16 = jnp.bfloat16
F32 = jnp.float32
STACK = 4
TILE = 512
DIAGONAL = 256
LOAD_TILE = 1024
AHEAD = 4
MIB = 1024 * 1024


def trig(phase_index, extent):
    angles = phase_index.astype(np.float32) * np.float32(2.0 * math.pi / extent)
    norm_scale = np.float32(1.0 / math.sqrt(extent))
    return (
        (np.cos(angles) * norm_scale).astype(BF16).astype(np.float32),
        (np.sin(angles) * norm_scale).astype(BF16).astype(np.float32),
    )


def column_table(length, mode_count, owners):
    phase = np.arange(mode_count)[:, None] * np.arange(length)[None, :] % length
    cos_part, sin_part = trig(phase, length)
    both = np.stack([cos_part, -sin_part]).reshape(2, owners, mode_count // owners, length)
    return both.transpose(1, 0, 2, 3).reshape(2 * mode_count, length).astype(BF16)


def row_matrix(extent, mode_count):
    slot = np.arange(mode_count)
    frequency = np.where(slot < mode_count // 2, slot, extent - mode_count + slot)
    phase = frequency[:, None] * np.arange(extent)[None, :] % extent
    cos_part, sin_part = trig(phase, extent)
    return np.stack(
        [np.stack([cos_part, sin_part], 1), np.stack([-sin_part, cos_part], 1)], 1
    )


def split_rows(matrix, owners):
    rows, parts, extent = matrix.shape
    split = matrix.reshape(rows, parts, owners, extent // owners // 2, 2)
    split = split.transpose(4, 0, 1, 3, 2)
    return split.reshape(2, rows, parts * extent // 2)


def half_mask(shape):
    return lax.broadcasted_iota(jnp.int32, shape, len(shape) - 1) % LANES < LANES // 2


def fold(first, second):
    picked = jnp.where(half_mask(first.shape), first, second)
    return picked + pltpu.roll(picked, LANES // 2, 1)


def dot_nt(left, right):
    return lax.dot_general(left, right, (((1,), (1,)), ((), ())), preferred_element_type=F32)


def dot_nn(left, right):
    return jnp.dot(left, right, preferred_element_type=F32)


def weigh(values, mode_rows):
    row = lax.broadcasted_iota(jnp.int32, values.shape, 0)
    return jnp.where((row == 0) | (row == mode_rows), values, values * 2.0)


def tiles(length, size):
    return [slice(at, at + size) for at in range(0, length, size)]


class Loads:
    def __init__(self, pairs, sem_ref, size):
        self.copies = [
            [
                pltpu.make_async_copy(source.at[:, cols], target.at[:, cols], sem_ref.at[n, k])
                for n, (source, target) in enumerate(pairs)
            ]
            for k, cols in enumerate(tiles(pairs[0][0].shape[1], size))
        ]
        for k in range(AHEAD):
            self.start(k)

    def start(self, k):
        if k < len(self.copies):
            for copy in self.copies[k]:
                copy.start()

    def wait(self, k):
        for copy in self.copies[k]:
            copy.wait()
        self.start(k + AHEAD)


def columns_kernel(
    table_hbm, fields_hbm, upstream_hbm, weight_hbm,
    out_ref, fields_ref, table_ref, acc_ref, sem_ref,
):
    del upstream_hbm, weight_hbm
    parts = tiles(table_hbm.shape[1], LOAD_TILE)
    loads = Loads(((table_hbm, table_ref), (fields_hbm, fields_ref)), sem_ref, LOAD_TILE)
    for k, cols in enumerate(parts):
        loads.wait(k)
        product = dot_nt(table_ref[:, cols], fields_ref[:, cols])
        if k == 0:
            acc_ref[...] = product
        elif k < len(parts) - 1:
            acc_ref[...] += product
        else:
            out_ref[...] = (acc_ref[...] + product).reshape(out_ref.shape).astype(BF16)


def gather_rows(got_ref, flat_ref, z_ref):
    owners, slots, width = got_ref.shape
    mode_rows = slots // 2
    for h in range(width // LANES):
        part = got_ref[:, :, h * LANES : (h + 1) * LANES].astype(F32)
        flat_ref[h] = part.reshape(owners * slots, LANES)
    for p in range(2):
        for i in range(mode_rows):
            for h in range(width // LANES):
                block = flat_ref[h, pl.ds(p * mode_rows + i, owners, stride=slots), :]
                at = (p * (width // LANES) + h) * owners
                z_ref[i, at : at + owners, :] = block.astype(BF16)


def scatter_rows(values, flat_ref, i, owners, slots):
    mode_rows = slots // 2
    columns = flat_ref.shape[0]
    for p in range(2):
        for h in range(columns):
            at = (p * columns + h) * owners
            flat_ref[h, pl.ds(p * mode_rows + i, owners, stride=slots), :] = values[
                at : at + owners
            ]


def modes_kernel(
    place_ref, got_ref, weight_ref, rows_ref, back_ref, *rest, adjoint, samples
):
    given = samples if adjoint else 0
    x_refs, sent_ref, shared_refs = rest[:given], rest[given], rest[given + 1 : given + 1 + samples]
    flat_ref, z_ref, mode_ref, y_ref = rest[given + 1 + samples :]
    owners, slots, _ = got_ref.shape
    mode_rows, kx_count, channels, _ = weight_ref.shape
    gather_rows(got_ref, flat_ref, z_ref)
    count = 2 * kx_count
    stack_rows = 2 * STACK
    for i in range(mode_rows):
        z = z_ref[i]
        both = fold(dot_nn(rows_ref[0], z), dot_nn(rows_ref[1], z))
        if adjoint:
            plain, turned = both[:count], both[count:]
            left = jnp.where(half_mask(plain.shape), plain, turned)
            mode_ref[i] = left
            left = left.astype(BF16)
            row = lax.broadcasted_iota(jnp.int32, (stack_rows, LANES), 0) // 2
            low = half_mask((stack_rows, LANES))
            for g in range(kx_count // STACK):
                pair = left[g // 2 * 2 * stack_rows : (g // 2 + 1) * 2 * stack_rows]
                w = weight_ref[i, g * STACK : (g + 1) * STACK].reshape(STACK * channels, LANES)
                full = dot_nt(pair, w)[g % 2 * stack_rows : (g % 2 + 1) * stack_rows]
                picked = jnp.where(row < 2, full[:, :LANES], full[:, LANES:])
                picked = jnp.where((row % 2 == 0) == low, picked, 0.0)
                y_ref[g * stack_rows : (g + 1) * stack_rows, :] = picked + pltpu.roll(
                    picked, LANES // 2, 1
                )
        else:
            wide = jnp.concatenate([both, both], axis=1)
            lane = lax.broadcasted_iota(jnp.int32, wide.shape, 1) // channels
            row = lax.broadcasted_iota(jnp.int32, wide.shape, 0) % stack_rows // 2
            left = jnp.where(lane == row, wide, 0.0).astype(BF16)
            for g in range(kx_count // STACK):
                rows = slice(g * 2 * stack_rows, (g + 1) * 2 * stack_rows)
                mode_ref[i, g * stack_rows : (g + 1) * stack_rows, :] = both[rows][:stack_rows]
                w = weight_ref[i, g * STACK : (g + 1) * STACK].reshape(STACK * channels, LANES)
                full = dot_nn(left[rows], w)
                y_ref[g * stack_rows : (g + 1) * stack_rows, :] = fold(
                    full[:stack_rows], full[stack_rows:]
                )
        y = y_ref[...].astype(BF16)
        low = half_mask((back_ref.shape[1], LANES))
        values = jnp.where(low, dot_nn(back_ref[0], y), dot_nn(back_ref[1], y))
        scatter_rows(values, flat_ref, i, owners, slots)
    for h in range(flat_ref.shape[0]):
        part = flat_ref[h].reshape(owners, slots, LANES)
        sent_ref[:, :, h * LANES : (h + 1) * LANES] = part.astype(BF16)
    block = count // samples
    for k, shared_ref in enumerate(shared_refs):
        start = pl.multiple_of((place_ref[0] + k) % samples * block, block)
        if adjoint:
            shared_ref[0] = x_refs[k][...]
        for i in range(mode_rows):
            values = mode_ref[i, pl.ds(start, block), :].astype(BF16)
            if adjoint:
                shared_ref[1, i] = values
            else:
                shared_ref[i] = values


def transposed_back(back_ref, mode_rows, weighted):
    owners, slots, width = back_ref.shape
    flat = back_ref[...].astype(F32).reshape(owners * slots, width)
    if weighted:
        flat = weigh(flat, mode_rows)
    return flat.T.astype(BF16)


def spread(block, out_ref):
    out_ref[...] = jnp.zeros_like(out_ref)
    size = block.shape[0]
    for at in range(0, out_ref.shape[0], size):
        out_ref[at : at + size, at : at + size] = block


def gelu_chunk(pre_ref, upstream_ref, response_ref, delta_ref, slot, rows, cols):
    v = pre_ref[slot, rows, :]
    t = jnp.tanh(v * (GELU_SCALE + (GELU_SCALE * GELU_CUBIC) * (v * v)))
    half = (0.5 + 0.5 * t).astype(BF16)
    rest = (1.0 - t * t).astype(BF16)
    v = v.astype(BF16)
    response_ref[rows, cols] = v * half
    inner = (0.5 * GELU_SCALE) + (1.5 * GELU_SCALE * GELU_CUBIC) * (v * v)
    delta_ref[rows, cols] = upstream_ref[rows, cols] * (half + v * rest * inner)


def field_kernel(
    back_ref, table_ref, fields_ref, upstream_ref, weight_ref,
    response_hbm, delta_hbm, sent_ref,
    response_ref, delta_ref, turned_ref, mix_ref, pre_ref, acc_ref, sem_ref,
):
    mode_rows = back_ref.shape[1] // 2
    turned_ref[...] = transposed_back(back_ref, mode_rows, True)
    spread(weight_ref[...].astype(F32).T.astype(BF16), mix_ref)
    width = mix_ref.shape[0]
    total = fields_ref.shape[0]
    chunk = 32
    parts = tiles(table_ref.shape[1], TILE)
    copies = []

    def preact(k, at):
        rows = slice(at, at + width)
        pre_ref[k % 2, rows, :] = dot_nn(turned_ref[rows, :], table_ref[:, parts[k]]) + dot_nn(
            mix_ref[...], fields_ref[rows, parts[k]]
        )

    for at in range(0, total, width):
        preact(0, at)
    for k, cols in enumerate(parts):
        for at in range(0, total, chunk):
            if at % width == 0 and k + 1 < len(parts):
                preact(k + 1, at)
            rows = slice(at, at + chunk)
            gelu_chunk(pre_ref, upstream_ref, response_ref, delta_ref, k % 2, rows, cols)
        for n, (source, target) in enumerate(
            ((response_ref, response_hbm), (delta_ref, delta_hbm))
        ):
            copies.append(
                pltpu.make_async_copy(
                    source.at[:, cols], target.at[:, cols], sem_ref.at[n, k]
                )
            )
            copies[-1].start()
        product = dot_nt(table_ref[:, cols], delta_ref[:, cols])
        if k == 0:
            acc_ref[...] = product
        elif k < len(parts) - 1:
            acc_ref[...] += product
        else:
            sent = weigh(acc_ref[...] + product, mode_rows)
            sent_ref[...] = sent.reshape(sent_ref.shape).astype(BF16)
    for copy in copies:
        copy.wait()


def mode_products(shared_refs, out_ref, i):
    _, kx_here, channels, _ = out_ref.shape
    stack_rows = 2 * STACK
    count = len(shared_refs) * stack_rows
    row = lax.broadcasted_iota(jnp.int32, (count, LANES), 0) % stack_rows // 2
    for g in range(kx_here // STACK):
        rows = slice(g * stack_rows, (g + 1) * stack_rows)
        x = jnp.concatenate([ref[0, i, rows, :].astype(F32) for ref in shared_refs], axis=0)
        d = jnp.concatenate([ref[1, i, rows, :].astype(F32) for ref in shared_refs], axis=0)
        wide = jnp.concatenate([jnp.where(row == m, d, 0.0) for m in range(STACK)], axis=1)
        product = dot_nn(x.T[:channels].astype(BF16), wide.astype(BF16))
        for m in range(STACK):
            out_ref[i, g * STACK + m] = product[:, m * LANES : (m + 1) * LANES]


def grad_kernel(back_ref, table_ref, delta_hbm, weight_ref, *rest, samples):
    shared_refs, (out_hbm, modes_hbm) = rest[:samples], rest[samples : samples + 2]
    delta_ref, turned_ref, mix_ref, out_ref, modes_ref, sem_ref = rest[samples + 2 :]
    loads = Loads(((delta_hbm, delta_ref),), sem_ref, LOAD_TILE)
    turned_ref[...] = transposed_back(back_ref, 0, False)
    spread(weight_ref[...], mix_ref)
    width = mix_ref.shape[0]
    copies = []
    for i in range(modes_ref.shape[0]):
        mode_products(shared_refs, modes_ref, i)
        copies.append(pltpu.make_async_copy(modes_ref.at[i], modes_hbm.at[i], sem_ref.at[2, i]))
        copies[-1].start()
    for k, cols in enumerate(tiles(table_ref.shape[1], LOAD_TILE)):
        loads.wait(k)
        for at in range(0, delta_ref.shape[0], width):
            rows = slice(at, at + width)
            out_ref[rows, cols] = (
                dot_nn(turned_ref[rows, :], table_ref[:, cols])
                + dot_nn(mix_ref[...], delta_ref[rows, cols])
            ).astype(BF16)
        copies.append(
            pltpu.make_async_copy(out_ref.at[:, cols], out_hbm.at[:, cols], sem_ref.at[1, k])
        )
        copies[-1].start()
    for copy in copies:
        copy.wait()


VMEM = pl.BlockSpec(memory_space=pltpu.VMEM)
HBM = pl.BlockSpec(memory_space=pltpu.HBM)


def pinned(values):
    return pltpu.with_memory_space_constraint(values, pltpu.HBM)


def cost(mib):
    return pl.CostEstimate(flops=0, transcendentals=0, bytes_accessed=mib * MIB)


def params(mib):
    return pltpu.CompilerParams(vmem_limit_bytes=mib * MIB)


def on_device(fields, cotangent, mode_weight, mix_weight):
    _, rows_here, channels, length = fields.shape
    mode_rows, kx_count = mode_weight.shape[:2]
    groups = lax.axis_size("space")
    samples = lax.axis_size("dp")
    ky_count = mode_rows * groups
    extent = rows_here * groups
    lines = rows_here * channels
    slots = 2 * mode_rows
    signal = fields.reshape(lines, length)
    upstream = cotangent.reshape(lines, length)
    table = jnp.asarray(column_table(length, ky_count, groups))
    matrix = row_matrix(extent, kx_count)
    turned = np.stack([-matrix[:, 1], matrix[:, 0]], 1)
    plain_rows = matrix.reshape(2 * kx_count, 2, extent)
    turned_rows = turned.reshape(2 * kx_count, 2, extent)
    grouped = np.concatenate(
        [
            part.reshape(kx_count // STACK, 2 * STACK, 2, extent)
            for part in (plain_rows, turned_rows)
        ],
        axis=1,
    ).reshape(4 * kx_count, 2, extent)
    mix_rows = jnp.asarray(split_rows(grouped, groups).astype(BF16))
    adjoint_rows = jnp.asarray(
        split_rows(np.concatenate([plain_rows, -turned_rows]), groups).astype(BF16)
    )
    back_rows = jnp.asarray(
        split_rows(plain_rows, groups).transpose(0, 2, 1).astype(BF16)
    )
    place = lax.axis_index("dp").astype(jnp.int32).reshape(1)

    exchange_shape = jax.ShapeDtypeStruct((groups, slots, lines), BF16)
    lines_shape = pltpu.HBM((lines, length), BF16)
    steps = length // TILE

    def exchange(values):
        return lax.all_to_all(values, "space", 0, 0, tiled=True)

    def mix(got, rows, given):
        adjoint = bool(given)
        shape = (mode_rows, 2 * kx_count // samples, LANES)
        block = jax.ShapeDtypeStruct((2,) + shape if adjoint else shape, BF16)
        outs = pl.pallas_call(
            lambda *refs: modes_kernel(*refs, adjoint=adjoint, samples=samples),
            out_shape=[exchange_shape] + [block] * samples,
            in_specs=[pl.BlockSpec(memory_space=pltpu.SMEM)] + [VMEM] * (4 + len(given)),
            out_specs=[VMEM] * (1 + samples),
            scratch_shapes=[
                pltpu.VMEM((lines // LANES, groups * slots, LANES), F32),
                pltpu.VMEM((mode_rows, rows_here * groups, LANES), BF16),
                pltpu.VMEM((mode_rows, 2 * kx_count, LANES), F32),
                pltpu.VMEM((2 * kx_count, LANES), F32),
            ],
            compiler_params=params(10),
            cost_estimate=cost(16),
            name="adjoint_modes" if adjoint else "mix_modes",
        )(place, got, mode_weight, rows, back_rows, *given)
        return outs[0], outs[1:]

    def share(blocks):
        return [blocks[0]] + [
            lax.ppermute(
                blocks[k], "dp", [(a, (a + k) % samples) for a in range(samples)]
            )
            for k in range(1, samples)
        ]

    columns, near_signal = pl.pallas_call(
        columns_kernel,
        out_shape=[exchange_shape, jax.ShapeDtypeStruct((lines, length), BF16)],
        in_specs=[HBM] * 4,
        out_specs=[VMEM, VMEM],
        scratch_shapes=[
            pltpu.VMEM(table.shape, BF16),
            pltpu.VMEM((2 * ky_count, lines), F32),
            pltpu.SemaphoreType.DMA((2, length // LOAD_TILE)),
        ],
        compiler_params=params(14),
        cost_estimate=cost(16),
        name="columns",
    )(pinned(table), pinned(signal), pinned(upstream), pinned(mode_weight))
    columns, place = lax.optimization_barrier((columns, place))
    sent, spectrum = mix(exchange(columns), mix_rows, ())
    back = exchange(sent)
    response, delta, delta_columns = pl.pallas_call(
        field_kernel,
        out_shape=[lines_shape, lines_shape, exchange_shape],
        in_specs=[VMEM] * 5,
        out_specs=[HBM, HBM, VMEM],
        scratch_shapes=[pltpu.VMEM((lines, length), BF16)] * 2
        + [
            pltpu.VMEM((lines, 2 * ky_count), BF16),
            pltpu.VMEM((DIAGONAL, DIAGONAL), BF16),
            pltpu.VMEM((2, lines, TILE), F32),
            pltpu.VMEM((2 * ky_count, lines), F32),
            pltpu.SemaphoreType.DMA((2, steps)),
        ],
        compiler_params=params(20),
        cost_estimate=cost(24),
        name="field_step",
    )(back, table, near_signal, upstream, mix_weight)
    sent, both_modes = mix(exchange(delta_columns), adjoint_rows, spectrum)
    shared = share(both_modes)
    back = exchange(sent)
    modes_shape = pltpu.HBM((mode_rows, kx_count // samples, channels, LANES), F32)
    field_grad, mode_grad = pl.pallas_call(
        lambda *refs: grad_kernel(*refs, samples=samples),
        out_shape=[lines_shape, modes_shape],
        in_specs=[VMEM, VMEM, HBM, VMEM] + [VMEM] * samples,
        out_specs=[HBM, HBM],
        scratch_shapes=[
            pltpu.VMEM((lines, length), BF16),
            pltpu.VMEM((lines, 2 * ky_count), BF16),
            pltpu.VMEM((DIAGONAL, DIAGONAL), BF16),
            pltpu.VMEM((lines, length), BF16),
            pltpu.VMEM(modes_shape.shape, F32),
            pltpu.SemaphoreType.DMA((3, max(length // LOAD_TILE, mode_rows))),
        ],
        compiler_params=params(20),
        cost_estimate=cost(16),
        name="gradients",
    )(back, table, pinned(delta), mix_weight, *shared)
    return (response.reshape(fields.shape), field_grad.reshape(fields.shape), mode_grad)


def solution(mesh):
    in_specs = (
        P("dp", "space", None, None),
        P("dp", "space", None, None),
        P("space", None, None, None),
        P(),
    )
    out_specs = (
        P("dp", "space", None, None),
        P("dp", "space", None, None),
        P("space", "dp", None, None),
    )
    return jax.shard_map(
        on_device, mesh=mesh, in_specs=in_specs, out_specs=out_specs, check_vma=False
    )
```

```python
import math

import jax
import jax.numpy as jnp
import numpy as np
from jax import lax
from jax.experimental import pallas as pl
from jax.experimental.pallas import tpu as pltpu
from jax.sharding import PartitionSpec as P

GELU_CUBIC = 0.044715
GELU_SCALE = math.sqrt(2.0 / math.pi)
LANES = 128
BF16 = jnp.bfloat16
F32 = jnp.float32
STACK = 4
TILE = 512
DIAGONAL = 256
LOAD_TILE = 1024
AHEAD = 4
MIB = 1024 * 1024


def trig(phase_index, extent):
    angles = phase_index.astype(np.float32) * np.float32(2.0 * math.pi / extent)
    norm_scale = np.float32(1.0 / math.sqrt(extent))
    return (
        (np.cos(angles) * norm_scale).astype(BF16).astype(np.float32),
        (np.sin(angles) * norm_scale).astype(BF16).astype(np.float32),
    )


def column_table(length, mode_count, owners):
    phase = np.arange(mode_count)[:, None] * np.arange(length)[None, :] % length
    cos_part, sin_part = trig(phase, length)
    both = np.stack([cos_part, -sin_part]).reshape(2, owners, mode_count // owners, length)
    return both.transpose(1, 0, 2, 3).reshape(2 * mode_count, length).astype(BF16)


def row_matrix(extent, mode_count):
    slot = np.arange(mode_count)
    frequency = np.where(slot < mode_count // 2, slot, extent - mode_count + slot)
    phase = frequency[:, None] * np.arange(extent)[None, :] % extent
    cos_part, sin_part = trig(phase, extent)
    return np.stack(
        [np.stack([cos_part, sin_part], 1), np.stack([-sin_part, cos_part], 1)], 1
    )


def split_rows(matrix, owners):
    rows, parts, extent = matrix.shape
    split = matrix.reshape(rows, parts, owners, extent // owners // 2, 2)
    split = split.transpose(4, 0, 1, 3, 2)
    return split.reshape(2, rows, parts * extent // 2)


def half_mask(shape):
    return lax.broadcasted_iota(jnp.int32, shape, len(shape) - 1) % LANES < LANES // 2


def fold(first, second):
    picked = jnp.where(half_mask(first.shape), first, second)
    return picked + pltpu.roll(picked, LANES // 2, 1)


def dot_nt(left, right):
    return lax.dot_general(left, right, (((1,), (1,)), ((), ())), preferred_element_type=F32)


def dot_nn(left, right):
    return jnp.dot(left, right, preferred_element_type=F32)


def weigh(values, mode_rows):
    row = lax.broadcasted_iota(jnp.int32, values.shape, 0)
    return jnp.where((row == 0) | (row == mode_rows), values, values * 2.0)


def tiles(length, size):
    return [slice(at, at + size) for at in range(0, length, size)]


class Loads:
    def __init__(self, pairs, sem_ref, size):
        self.copies = [
            [
                pltpu.make_async_copy(source.at[:, cols], target.at[:, cols], sem_ref.at[n, k])
                for n, (source, target) in enumerate(pairs)
            ]
            for k, cols in enumerate(tiles(pairs[0][0].shape[1], size))
        ]
        for k in range(AHEAD):
            self.start(k)

    def start(self, k):
        if k < len(self.copies):
            for copy in self.copies[k]:
                copy.start()

    def wait(self, k):
        for copy in self.copies[k]:
            copy.wait()
        self.start(k + AHEAD)


def columns_kernel(
    table_hbm, fields_hbm, upstream_hbm, weight_hbm,
    out_ref, fields_ref, table_ref, acc_ref, sem_ref,
):
    del upstream_hbm, weight_hbm
    parts = tiles(table_hbm.shape[1], LOAD_TILE)
    loads = Loads(((table_hbm, table_ref), (fields_hbm, fields_ref)), sem_ref, LOAD_TILE)
    for k, cols in enumerate(parts):
        loads.wait(k)
        product = dot_nt(table_ref[:, cols], fields_ref[:, cols])
        if k == 0:
            acc_ref[...] = product
        elif k < len(parts) - 1:
            acc_ref[...] += product
        else:
            out_ref[...] = (acc_ref[...] + product).reshape(out_ref.shape).astype(BF16)


def gather_rows(got_ref, flat_ref, z_ref):
    owners, slots, width = got_ref.shape
    mode_rows = slots // 2
    for h in range(width // LANES):
        part = got_ref[:, :, h * LANES : (h + 1) * LANES].astype(F32)
        flat_ref[h] = part.reshape(owners * slots, LANES)
    for p in range(2):
        for i in range(mode_rows):
            for h in range(width // LANES):
                block = flat_ref[h, pl.ds(p * mode_rows + i, owners, stride=slots), :]
                at = (p * (width // LANES) + h) * owners
                z_ref[at : at + owners, i * LANES : (i + 1) * LANES] = block.astype(BF16)


def scatter_rows(values, flat_ref, i, owners, slots):
    mode_rows = slots // 2
    columns = flat_ref.shape[0]
    for p in range(2):
        for h in range(columns):
            at = (p * columns + h) * owners
            flat_ref[h, pl.ds(p * mode_rows + i, owners, stride=slots), :] = values[
                at : at + owners
            ]


def modes_kernel(
    place_ref, got_ref, weight_ref, rows_ref, back_ref, *rest, adjoint, samples
):
    given = samples if adjoint else 0
    x_refs, sent_ref, shared_refs = rest[:given], rest[given], rest[given + 1 : given + 1 + samples]
    flat_ref, z_ref, mode_ref, y_ref = rest[given + 1 + samples :]
    owners, slots, _ = got_ref.shape
    mode_rows, kx_count, channels, _ = weight_ref.shape
    gather_rows(got_ref, flat_ref, z_ref)
    count = 2 * kx_count
    stack_rows = 2 * STACK
    first = dot_nn(rows_ref[0], z_ref[...])
    second = dot_nn(rows_ref[1], z_ref[...])
    for i in range(mode_rows):
        lanes = slice(i * LANES, (i + 1) * LANES)
        both = fold(first[:, lanes], second[:, lanes])
        if adjoint:
            plain, turned = both[:count], both[count:]
            left = jnp.where(half_mask(plain.shape), plain, turned)
            mode_ref[i] = left
            left = left.astype(BF16)
            row = lax.broadcasted_iota(jnp.int32, (stack_rows, LANES), 0) // 2
            low = half_mask((stack_rows, LANES))
            for g in range(kx_count // STACK):
                pair = left[g // 2 * 2 * stack_rows : (g // 2 + 1) * 2 * stack_rows]
                w = weight_ref[i, g * STACK : (g + 1) * STACK].reshape(STACK * channels, LANES)
                full = dot_nt(pair, w)[g % 2 * stack_rows : (g % 2 + 1) * stack_rows]
                picked = jnp.where(row < 2, full[:, :LANES], full[:, LANES:])
                picked = jnp.where((row % 2 == 0) == low, picked, 0.0)
                y_ref[g * stack_rows : (g + 1) * stack_rows, lanes] = picked + pltpu.roll(
                    picked, LANES // 2, 1
                )
        else:
            wide = jnp.concatenate([both, both], axis=1)
            lane = lax.broadcasted_iota(jnp.int32, wide.shape, 1) // channels
            row = lax.broadcasted_iota(jnp.int32, wide.shape, 0) % stack_rows // 2
            left = jnp.where(lane == row, wide, 0.0).astype(BF16)
            for g in range(kx_count // STACK):
                rows = slice(g * 2 * stack_rows, (g + 1) * 2 * stack_rows)
                mode_ref[i, g * stack_rows : (g + 1) * stack_rows, :] = both[rows][:stack_rows]
                w = weight_ref[i, g * STACK : (g + 1) * STACK].reshape(STACK * channels, LANES)
                full = dot_nn(left[rows], w)
                y_ref[g * stack_rows : (g + 1) * stack_rows, lanes] = fold(
                    full[:stack_rows], full[stack_rows:]
                )
    y = y_ref[...].astype(BF16)
    first, second = dot_nn(back_ref[0], y), dot_nn(back_ref[1], y)
    values = jnp.where(half_mask(first.shape), first, second)
    for i in range(mode_rows):
        scatter_rows(values[:, i * LANES : (i + 1) * LANES], flat_ref, i, owners, slots)
    for h in range(flat_ref.shape[0]):
        part = flat_ref[h].reshape(owners, slots, LANES)
        sent_ref[:, :, h * LANES : (h + 1) * LANES] = part.astype(BF16)
    block = count // samples
    for k, shared_ref in enumerate(shared_refs):
        start = pl.multiple_of((place_ref[0] + k) % samples * block, block)
        if adjoint:
            shared_ref[0] = x_refs[k][...]
        for i in range(mode_rows):
            values = mode_ref[i, pl.ds(start, block), :].astype(BF16)
            if adjoint:
                shared_ref[1, i] = values
            else:
                shared_ref[i] = values


def transposed_back(back_ref, mode_rows, weighted):
    owners, slots, width = back_ref.shape
    flat = back_ref[...].astype(F32).reshape(owners * slots, width)
    if weighted:
        flat = weigh(flat, mode_rows)
    return flat.T.astype(BF16)


def spread(block, out_ref):
    out_ref[...] = jnp.zeros_like(out_ref)
    size = block.shape[0]
    for at in range(0, out_ref.shape[0], size):
        out_ref[at : at + size, at : at + size] = block


def gelu_chunk(pre_ref, upstream_ref, response_ref, delta_ref, slot, rows, cols):
    v = pre_ref[slot, rows, :]
    t = jnp.tanh(v * (GELU_SCALE + (GELU_SCALE * GELU_CUBIC) * (v * v)))
    half = (0.5 + 0.5 * t).astype(BF16)
    rest = (1.0 - t * t).astype(BF16)
    v = v.astype(BF16)
    response_ref[rows, cols] = v * half
    inner = (0.5 * GELU_SCALE) + (1.5 * GELU_SCALE * GELU_CUBIC) * (v * v)
    delta_ref[rows, cols] = upstream_ref[rows, cols] * (half + v * rest * inner)


def field_kernel(
    back_ref, table_ref, fields_ref, upstream_ref, weight_ref,
    response_hbm, delta_hbm, sent_ref,
    response_ref, delta_ref, turned_ref, mix_ref, pre_ref, acc_ref, sem_ref,
):
    mode_rows = back_ref.shape[1] // 2
    turned_ref[...] = transposed_back(back_ref, mode_rows, True)
    spread(weight_ref[...].astype(F32).T.astype(BF16), mix_ref)
    width = mix_ref.shape[0]
    total = fields_ref.shape[0]
    chunk = 32
    parts = tiles(table_ref.shape[1], TILE)
    copies = []

    def preact(k, at):
        rows = slice(at, at + width)
        pre_ref[k % 2, rows, :] = dot_nn(turned_ref[rows, :], table_ref[:, parts[k]]) + dot_nn(
            mix_ref[...], fields_ref[rows, parts[k]]
        )

    for at in range(0, total, width):
        preact(0, at)
    for k, cols in enumerate(parts):
        for at in range(0, total, chunk):
            if at % width == 0 and k + 1 < len(parts):
                preact(k + 1, at)
            rows = slice(at, at + chunk)
            gelu_chunk(pre_ref, upstream_ref, response_ref, delta_ref, k % 2, rows, cols)
        for n, (source, target) in enumerate(
            ((response_ref, response_hbm), (delta_ref, delta_hbm))
        ):
            copies.append(
                pltpu.make_async_copy(
                    source.at[:, cols], target.at[:, cols], sem_ref.at[n, k]
                )
            )
            copies[-1].start()
        product = dot_nt(table_ref[:, cols], delta_ref[:, cols])
        if k == 0:
            acc_ref[...] = product
        elif k < len(parts) - 1:
            acc_ref[...] += product
        else:
            sent = weigh(acc_ref[...] + product, mode_rows)
            sent_ref[...] = sent.reshape(sent_ref.shape).astype(BF16)
    for copy in copies:
        copy.wait()


def mode_products(shared_refs, out_ref, i):
    _, kx_here, channels, _ = out_ref.shape
    stack_rows = 2 * STACK
    count = len(shared_refs) * stack_rows
    row = lax.broadcasted_iota(jnp.int32, (count, LANES), 0) % stack_rows // 2
    for g in range(kx_here // STACK):
        rows = slice(g * stack_rows, (g + 1) * stack_rows)
        x = jnp.concatenate([ref[0, i, rows, :].astype(F32) for ref in shared_refs], axis=0)
        d = jnp.concatenate([ref[1, i, rows, :].astype(F32) for ref in shared_refs], axis=0)
        wide = jnp.concatenate([jnp.where(row == m, d, 0.0) for m in range(STACK)], axis=1)
        product = dot_nn(x.T[:channels].astype(BF16), wide.astype(BF16))
        for m in range(STACK):
            out_ref[i, g * STACK + m] = product[:, m * LANES : (m + 1) * LANES]


def grad_kernel(back_ref, table_ref, delta_hbm, weight_ref, *rest, samples):
    shared_refs, (out_hbm, modes_hbm) = rest[:samples], rest[samples : samples + 2]
    delta_ref, turned_ref, mix_ref, out_ref, modes_ref, sem_ref = rest[samples + 2 :]
    loads = Loads(((delta_hbm, delta_ref),), sem_ref, LOAD_TILE)
    turned_ref[...] = transposed_back(back_ref, 0, False)
    spread(weight_ref[...], mix_ref)
    width = mix_ref.shape[0]
    copies = []
    for i in range(modes_ref.shape[0]):
        mode_products(shared_refs, modes_ref, i)
        copies.append(pltpu.make_async_copy(modes_ref.at[i], modes_hbm.at[i], sem_ref.at[2, i]))
        copies[-1].start()
    for k, cols in enumerate(tiles(table_ref.shape[1], LOAD_TILE)):
        loads.wait(k)
        for at in range(0, delta_ref.shape[0], width):
            rows = slice(at, at + width)
            out_ref[rows, cols] = (
                dot_nn(turned_ref[rows, :], table_ref[:, cols])
                + dot_nn(mix_ref[...], delta_ref[rows, cols])
            ).astype(BF16)
        copies.append(
            pltpu.make_async_copy(out_ref.at[:, cols], out_hbm.at[:, cols], sem_ref.at[1, k])
        )
        copies[-1].start()
    for copy in copies:
        copy.wait()


VMEM = pl.BlockSpec(memory_space=pltpu.VMEM)
HBM = pl.BlockSpec(memory_space=pltpu.HBM)


def pinned(values):
    return pltpu.with_memory_space_constraint(values, pltpu.HBM)


def cost(mib):
    return pl.CostEstimate(flops=0, transcendentals=0, bytes_accessed=mib * MIB)


def params(mib):
    return pltpu.CompilerParams(vmem_limit_bytes=mib * MIB)


def on_device(fields, cotangent, mode_weight, mix_weight):
    _, rows_here, channels, length = fields.shape
    mode_rows, kx_count = mode_weight.shape[:2]
    groups = lax.axis_size("space")
    samples = lax.axis_size("dp")
    ky_count = mode_rows * groups
    extent = rows_here * groups
    lines = rows_here * channels
    slots = 2 * mode_rows
    signal = fields.reshape(lines, length)
    upstream = cotangent.reshape(lines, length)
    table = jnp.asarray(column_table(length, ky_count, groups))
    matrix = row_matrix(extent, kx_count)
    turned = np.stack([-matrix[:, 1], matrix[:, 0]], 1)
    plain_rows = matrix.reshape(2 * kx_count, 2, extent)
    turned_rows = turned.reshape(2 * kx_count, 2, extent)
    grouped = np.concatenate(
        [
            part.reshape(kx_count // STACK, 2 * STACK, 2, extent)
            for part in (plain_rows, turned_rows)
        ],
        axis=1,
    ).reshape(4 * kx_count, 2, extent)
    mix_rows = jnp.asarray(split_rows(grouped, groups).astype(BF16))
    adjoint_rows = jnp.asarray(
        split_rows(np.concatenate([plain_rows, -turned_rows]), groups).astype(BF16)
    )
    back_rows = jnp.asarray(
        split_rows(plain_rows, groups).transpose(0, 2, 1).astype(BF16)
    )
    place = lax.axis_index("dp").astype(jnp.int32).reshape(1)

    exchange_shape = jax.ShapeDtypeStruct((groups, slots, lines), BF16)
    lines_shape = pltpu.HBM((lines, length), BF16)
    steps = length // TILE

    def exchange(values):
        return lax.all_to_all(values, "space", 0, 0, tiled=True)

    def mix(got, rows, given):
        adjoint = bool(given)
        shape = (mode_rows, 2 * kx_count // samples, LANES)
        block = jax.ShapeDtypeStruct((2,) + shape if adjoint else shape, BF16)
        outs = pl.pallas_call(
            lambda *refs: modes_kernel(*refs, adjoint=adjoint, samples=samples),
            out_shape=[exchange_shape] + [block] * samples,
            in_specs=[pl.BlockSpec(memory_space=pltpu.SMEM)] + [VMEM] * (4 + len(given)),
            out_specs=[VMEM] * (1 + samples),
            scratch_shapes=[
                pltpu.VMEM((lines // LANES, groups * slots, LANES), F32),
                pltpu.VMEM((rows_here * groups, mode_rows * LANES), BF16),
                pltpu.VMEM((mode_rows, 2 * kx_count, LANES), F32),
                pltpu.VMEM((2 * kx_count, mode_rows * LANES), F32),
            ],
            compiler_params=params(10),
            cost_estimate=cost(16),
            name="adjoint_modes" if adjoint else "mix_modes",
        )(place, got, mode_weight, rows, back_rows, *given)
        return outs[0], outs[1:]

    def share(blocks):
        return [blocks[0]] + [
            lax.ppermute(
                blocks[k], "dp", [(a, (a + k) % samples) for a in range(samples)]
            )
            for k in range(1, samples)
        ]

    columns, near_signal = pl.pallas_call(
        columns_kernel,
        out_shape=[exchange_shape, jax.ShapeDtypeStruct((lines, length), BF16)],
        in_specs=[HBM] * 4,
        out_specs=[VMEM, VMEM],
        scratch_shapes=[
            pltpu.VMEM(table.shape, BF16),
            pltpu.VMEM((2 * ky_count, lines), F32),
            pltpu.SemaphoreType.DMA((2, length // LOAD_TILE)),
        ],
        compiler_params=params(14),
        cost_estimate=cost(16),
        name="columns",
    )(pinned(table), pinned(signal), pinned(upstream), pinned(mode_weight))
    columns, place = lax.optimization_barrier((columns, place))
    sent, spectrum = mix(exchange(columns), mix_rows, ())
    back = exchange(sent)
    response, delta, delta_columns = pl.pallas_call(
        field_kernel,
        out_shape=[lines_shape, lines_shape, exchange_shape],
        in_specs=[VMEM] * 5,
        out_specs=[HBM, HBM, VMEM],
        scratch_shapes=[pltpu.VMEM((lines, length), BF16)] * 2
        + [
            pltpu.VMEM((lines, 2 * ky_count), BF16),
            pltpu.VMEM((DIAGONAL, DIAGONAL), BF16),
            pltpu.VMEM((2, lines, TILE), F32),
            pltpu.VMEM((2 * ky_count, lines), F32),
            pltpu.SemaphoreType.DMA((2, steps)),
        ],
        compiler_params=params(20),
        cost_estimate=cost(24),
        name="field_step",
    )(back, table, near_signal, upstream, mix_weight)
    sent, both_modes = mix(exchange(delta_columns), adjoint_rows, spectrum)
    shared = share(both_modes)
    back = exchange(sent)
    modes_shape = pltpu.HBM((mode_rows, kx_count // samples, channels, LANES), F32)
    field_grad, mode_grad = pl.pallas_call(
        lambda *refs: grad_kernel(*refs, samples=samples),
        out_shape=[lines_shape, modes_shape],
        in_specs=[VMEM, VMEM, HBM, VMEM] + [VMEM] * samples,
        out_specs=[HBM, HBM],
        scratch_shapes=[
            pltpu.VMEM((lines, length), BF16),
            pltpu.VMEM((lines, 2 * ky_count), BF16),
            pltpu.VMEM((DIAGONAL, DIAGONAL), BF16),
            pltpu.VMEM((lines, length), BF16),
            pltpu.VMEM(modes_shape.shape, F32),
            pltpu.SemaphoreType.DMA((3, max(length // LOAD_TILE, mode_rows))),
        ],
        compiler_params=params(20),
        cost_estimate=cost(16),
        name="gradients",
    )(back, table, pinned(delta), mix_weight, *shared)
    return (response.reshape(fields.shape), field_grad.reshape(fields.shape), mode_grad)


def solution(mesh):
    in_specs = (
        P("dp", "space", None, None),
        P("dp", "space", None, None),
        P("space", None, None, None),
        P(),
    )
    out_specs = (
        P("dp", "space", None, None),
        P("dp", "space", None, None),
        P("space", "dp", None, None),
    )
    return jax.shard_map(
        on_device, mesh=mesh, in_specs=in_specs, out_specs=out_specs, check_vma=False
    )
```

```python
import math

import jax
import jax.numpy as jnp
import numpy as np
from jax import lax
from jax.experimental import pallas as pl
from jax.experimental.pallas import tpu as pltpu
from jax.sharding import PartitionSpec as P

GELU_CUBIC = 0.044715
GELU_SCALE = math.sqrt(2.0 / math.pi)
LANES = 128
BF16 = jnp.bfloat16
F32 = jnp.float32
STACK = 4
TILE = 512
DIAGONAL = 256
LOAD_TILE = 1024
AHEAD = 4
MIB = 1024 * 1024


def trig(phase_index, extent):
    angles = phase_index.astype(np.float32) * np.float32(2.0 * math.pi / extent)
    norm_scale = np.float32(1.0 / math.sqrt(extent))
    return (
        (np.cos(angles) * norm_scale).astype(BF16).astype(np.float32),
        (np.sin(angles) * norm_scale).astype(BF16).astype(np.float32),
    )


def column_table(length, mode_count, owners):
    phase = np.arange(mode_count)[:, None] * np.arange(length)[None, :] % length
    cos_part, sin_part = trig(phase, length)
    both = np.stack([cos_part, -sin_part]).reshape(2, owners, mode_count // owners, length)
    return both.transpose(1, 0, 2, 3).reshape(2 * mode_count, length).astype(BF16)


def row_matrix(extent, mode_count):
    slot = np.arange(mode_count)
    frequency = np.where(slot < mode_count // 2, slot, extent - mode_count + slot)
    phase = frequency[:, None] * np.arange(extent)[None, :] % extent
    cos_part, sin_part = trig(phase, extent)
    return np.stack(
        [np.stack([cos_part, sin_part], 1), np.stack([-sin_part, cos_part], 1)], 1
    )


def split_rows(matrix, owners):
    rows, parts, extent = matrix.shape
    split = matrix.reshape(rows, parts, owners, extent // owners // 2, 2)
    split = split.transpose(4, 0, 1, 3, 2)
    return split.reshape(2, rows, parts * extent // 2)


def half_mask(shape):
    return lax.broadcasted_iota(jnp.int32, shape, len(shape) - 1) % LANES < LANES // 2


def fold(first, second):
    picked = jnp.where(half_mask(first.shape), first, second)
    return picked + pltpu.roll(picked, LANES // 2, 1)


def dot_nt(left, right):
    return lax.dot_general(left, right, (((1,), (1,)), ((), ())), preferred_element_type=F32)


def dot_nn(left, right):
    return jnp.dot(left, right, preferred_element_type=F32)


def weigh(values, mode_rows):
    row = lax.broadcasted_iota(jnp.int32, values.shape, 0)
    return jnp.where((row == 0) | (row == mode_rows), values, values * 2.0)


def tiles(length, size):
    return [slice(at, at + size) for at in range(0, length, size)]


class Loads:
    def __init__(self, pairs, sem_ref, size):
        self.copies = [
            [
                pltpu.make_async_copy(source.at[:, cols], target.at[:, cols], sem_ref.at[n, k])
                for n, (source, target) in enumerate(pairs)
            ]
            for k, cols in enumerate(tiles(pairs[0][0].shape[1], size))
        ]
        for k in range(AHEAD):
            self.start(k)

    def start(self, k):
        if k < len(self.copies):
            for copy in self.copies[k]:
                copy.start()

    def wait(self, k):
        for copy in self.copies[k]:
            copy.wait()
        self.start(k + AHEAD)


def columns_kernel(
    table_hbm, fields_hbm, upstream_hbm, weight_hbm,
    out_ref, fields_ref, table_ref, acc_ref, sem_ref,
):
    del upstream_hbm, weight_hbm
    parts = tiles(table_hbm.shape[1], LOAD_TILE)
    loads = Loads(((table_hbm, table_ref), (fields_hbm, fields_ref)), sem_ref, LOAD_TILE)
    for k, cols in enumerate(parts):
        loads.wait(k)
        product = dot_nt(table_ref[:, cols], fields_ref[:, cols])
        if k == 0:
            acc_ref[...] = product
        elif k < len(parts) - 1:
            acc_ref[...] += product
        else:
            out_ref[...] = (acc_ref[...] + product).reshape(out_ref.shape).astype(BF16)


def gather_rows(got_ref, flat_ref, z_ref):
    owners, slots, width = got_ref.shape
    mode_rows = slots // 2
    for h in range(width // LANES):
        part = got_ref[:, :, h * LANES : (h + 1) * LANES].astype(F32)
        flat_ref[h] = part.reshape(owners * slots, LANES)
    for p in range(2):
        for i in range(mode_rows):
            for h in range(width // LANES):
                block = flat_ref[h, pl.ds(p * mode_rows + i, owners, stride=slots), :]
                at = (p * (width // LANES) + h) * owners
                z_ref[at : at + owners, i * LANES : (i + 1) * LANES] = block.astype(BF16)


def scatter_rows(values, flat_ref, i, owners, slots):
    mode_rows = slots // 2
    columns = flat_ref.shape[0]
    for p in range(2):
        for h in range(columns):
            at = (p * columns + h) * owners
            flat_ref[h, pl.ds(p * mode_rows + i, owners, stride=slots), :] = values[
                at : at + owners
            ]


def modes_kernel(
    place_ref, got_ref, weight_ref, rows_ref, back_ref, *rest, adjoint, samples
):
    given = samples if adjoint else 0
    x_refs, sent_ref, shared_refs = rest[:given], rest[given], rest[given + 1 : given + 1 + samples]
    flat_ref, z_ref, mode_ref, y_ref = rest[given + 1 + samples :]
    owners, slots, _ = got_ref.shape
    mode_rows, kx_count, channels, _ = weight_ref.shape
    gather_rows(got_ref, flat_ref, z_ref)
    count = 2 * kx_count
    stack_rows = 2 * STACK
    first = dot_nn(rows_ref[0], z_ref[...])
    second = dot_nn(rows_ref[1], z_ref[...])
    for i in range(mode_rows):
        lanes = slice(i * LANES, (i + 1) * LANES)
        both = fold(first[:, lanes], second[:, lanes])
        if adjoint:
            plain, turned = both[:count], both[count:]
            left = jnp.where(half_mask(plain.shape), plain, turned)
            mode_ref[i] = left
            left = left.astype(BF16)
            row = lax.broadcasted_iota(jnp.int32, (stack_rows, LANES), 0) // 2
            low = half_mask((stack_rows, LANES))
            for g in range(kx_count // STACK):
                pair = left[g // 2 * 2 * stack_rows : (g // 2 + 1) * 2 * stack_rows]
                w = weight_ref[i, g * STACK : (g + 1) * STACK].reshape(STACK * channels, LANES)
                full = dot_nt(pair, w)[g % 2 * stack_rows : (g % 2 + 1) * stack_rows]
                picked = jnp.where(row < 2, full[:, :LANES], full[:, LANES:])
                picked = jnp.where((row % 2 == 0) == low, picked, 0.0)
                y_ref[g * stack_rows : (g + 1) * stack_rows, lanes] = picked + pltpu.roll(
                    picked, LANES // 2, 1
                )
        else:
            wide = jnp.concatenate([both, both], axis=1)
            lane = lax.broadcasted_iota(jnp.int32, wide.shape, 1) // channels
            row = lax.broadcasted_iota(jnp.int32, wide.shape, 0) % stack_rows // 2
            left = jnp.where(lane == row, wide, 0.0).astype(BF16)
            for g in range(kx_count // STACK):
                rows = slice(g * 2 * stack_rows, (g + 1) * 2 * stack_rows)
                mode_ref[i, g * stack_rows : (g + 1) * stack_rows, :] = both[rows][:stack_rows]
                w = weight_ref[i, g * STACK : (g + 1) * STACK].reshape(STACK * channels, LANES)
                full = dot_nn(left[rows], w)
                y_ref[g * stack_rows : (g + 1) * stack_rows, lanes] = fold(
                    full[:stack_rows], full[stack_rows:]
                )
    y = y_ref[...].astype(BF16)
    first, second = dot_nn(back_ref[0], y), dot_nn(back_ref[1], y)
    values = jnp.where(half_mask(first.shape), first, second)
    for i in range(mode_rows):
        scatter_rows(values[:, i * LANES : (i + 1) * LANES], flat_ref, i, owners, slots)
    for h in range(flat_ref.shape[0]):
        part = flat_ref[h].reshape(owners, slots, LANES)
        sent_ref[:, :, h * LANES : (h + 1) * LANES] = part.astype(BF16)
    block = count // samples
    for k, shared_ref in enumerate(shared_refs):
        start = pl.multiple_of((place_ref[0] + k) % samples * block, block)
        if adjoint:
            shared_ref[0] = x_refs[k][...]
        for i in range(mode_rows):
            values = mode_ref[i, pl.ds(start, block), :].astype(BF16)
            if adjoint:
                shared_ref[1, i] = values
            else:
                shared_ref[i] = values


def transpose_back(back_ref, turned_ref, mode_rows, weighted):
    owners, slots, width = back_ref.shape
    for at in range(0, width, DIAGONAL):
        flat = back_ref[:, :, at : at + DIAGONAL].astype(F32).reshape(owners * slots, DIAGONAL)
        if weighted:
            flat = weigh(flat, mode_rows)
        turned_ref[at : at + DIAGONAL, :] = flat.T.astype(BF16)


def spread(block, out_ref):
    out_ref[...] = jnp.zeros_like(out_ref)
    size = block.shape[0]
    for at in range(0, out_ref.shape[0], size):
        out_ref[at : at + size, at : at + size] = block


def gelu_chunk(pre_ref, upstream_ref, response_ref, delta_ref, slot, rows, cols):
    v = pre_ref[slot, rows, :]
    t = jnp.tanh(v * (GELU_SCALE + (GELU_SCALE * GELU_CUBIC) * (v * v)))
    scaled = 0.5 * t
    half = (0.5 + scaled).astype(BF16)
    other = (0.5 - scaled).astype(BF16)
    v = v.astype(BF16)
    value = v * half
    response_ref[rows, cols] = value
    inner = (2.0 * GELU_SCALE) + (6.0 * GELU_SCALE * GELU_CUBIC) * (v * v)
    delta_ref[rows, cols] = upstream_ref[rows, cols] * (half + value * other * inner)


def field_kernel(
    back_ref, table_ref, fields_ref, upstream_ref, weight_ref,
    response_hbm, delta_hbm, sent_ref,
    response_ref, delta_ref, turned_ref, mix_ref, pre_ref, acc_ref, sem_ref,
):
    mode_rows = back_ref.shape[1] // 2
    spread(weight_ref[...].astype(F32).T.astype(BF16), mix_ref)
    transpose_back(back_ref, turned_ref, mode_rows, True)
    width = mix_ref.shape[0]
    total = fields_ref.shape[0]
    chunk = 32
    parts = tiles(table_ref.shape[1], TILE)
    copies = []

    def preact(k, at):
        rows = slice(at, at + width)
        pre_ref[k % 2, rows, :] = dot_nn(turned_ref[rows, :], table_ref[:, parts[k]]) + dot_nn(
            mix_ref[...], fields_ref[rows, parts[k]]
        )

    for at in range(0, total, width):
        preact(0, at)
    for k, cols in enumerate(parts):
        for at in range(0, total, chunk):
            if at % width == 0 and k + 1 < len(parts):
                preact(k + 1, at)
            rows = slice(at, at + chunk)
            gelu_chunk(pre_ref, upstream_ref, response_ref, delta_ref, k % 2, rows, cols)
        for n, (source, target) in enumerate(
            ((response_ref, response_hbm), (delta_ref, delta_hbm))
        ):
            copies.append(
                pltpu.make_async_copy(
                    source.at[:, cols], target.at[:, cols], sem_ref.at[n, k]
                )
            )
            copies[-1].start()
        product = dot_nt(table_ref[:, cols], delta_ref[:, cols])
        if k == 0:
            acc_ref[...] = product
        elif k < len(parts) - 1:
            acc_ref[...] += product
        else:
            sent = weigh(acc_ref[...] + product, mode_rows)
            sent_ref[...] = sent.reshape(sent_ref.shape).astype(BF16)
    for copy in copies:
        copy.wait()


def mode_products(shared_refs, out_ref, i):
    _, kx_here, channels, _ = out_ref.shape
    stack_rows = 2 * STACK
    count = len(shared_refs) * stack_rows
    row = lax.broadcasted_iota(jnp.int32, (count, LANES), 0) % stack_rows // 2
    for g in range(kx_here // STACK):
        rows = slice(g * stack_rows, (g + 1) * stack_rows)
        x = jnp.concatenate([ref[0, i, rows, :].astype(F32) for ref in shared_refs], axis=0)
        d = jnp.concatenate([ref[1, i, rows, :].astype(F32) for ref in shared_refs], axis=0)
        wide = jnp.concatenate([jnp.where(row == m, d, 0.0) for m in range(STACK)], axis=1)
        product = dot_nn(x.T[:channels].astype(BF16), wide.astype(BF16))
        for m in range(STACK):
            out_ref[i, g * STACK + m] = product[:, m * LANES : (m + 1) * LANES]


def grad_kernel(back_ref, table_ref, delta_hbm, weight_ref, *rest, samples):
    shared_refs, (out_hbm, modes_hbm) = rest[:samples], rest[samples : samples + 2]
    delta_ref, turned_ref, mix_ref, out_ref, modes_ref, sem_ref = rest[samples + 2 :]
    loads = Loads(((delta_hbm, delta_ref),), sem_ref, LOAD_TILE)
    spread(weight_ref[...], mix_ref)
    transpose_back(back_ref, turned_ref, 0, False)
    width = mix_ref.shape[0]
    copies = []
    for i in range(modes_ref.shape[0]):
        mode_products(shared_refs, modes_ref, i)
        copies.append(pltpu.make_async_copy(modes_ref.at[i], modes_hbm.at[i], sem_ref.at[1, i]))
        copies[-1].start()
    for k, cols in enumerate(tiles(table_ref.shape[1], LOAD_TILE)):
        loads.wait(k)
        for n, at in enumerate(range(0, delta_ref.shape[0], width)):
            rows = slice(at, at + width)
            out_ref[rows, cols] = (
                dot_nn(turned_ref[rows, :], table_ref[:, cols])
                + dot_nn(mix_ref[...], delta_ref[rows, cols])
            ).astype(BF16)
            copies.append(
                pltpu.make_async_copy(
                    out_ref.at[rows, cols], out_hbm.at[rows, cols], sem_ref.at[2 + n, k]
                )
            )
            copies[-1].start()
    for copy in copies:
        copy.wait()


VMEM = pl.BlockSpec(memory_space=pltpu.VMEM)
HBM = pl.BlockSpec(memory_space=pltpu.HBM)


def pinned(values):
    return pltpu.with_memory_space_constraint(values, pltpu.HBM)


def cost(mib):
    return pl.CostEstimate(flops=0, transcendentals=0, bytes_accessed=mib * MIB)


def params(mib):
    return pltpu.CompilerParams(vmem_limit_bytes=mib * MIB)


def on_device(fields, cotangent, mode_weight, mix_weight):
    _, rows_here, channels, length = fields.shape
    mode_rows, kx_count = mode_weight.shape[:2]
    groups = lax.axis_size("space")
    samples = lax.axis_size("dp")
    ky_count = mode_rows * groups
    extent = rows_here * groups
    lines = rows_here * channels
    slots = 2 * mode_rows
    signal = fields.reshape(lines, length)
    upstream = cotangent.reshape(lines, length)
    table = jnp.asarray(column_table(length, ky_count, groups))
    matrix = row_matrix(extent, kx_count)
    turned = np.stack([-matrix[:, 1], matrix[:, 0]], 1)
    plain_rows = matrix.reshape(2 * kx_count, 2, extent)
    turned_rows = turned.reshape(2 * kx_count, 2, extent)
    grouped = np.concatenate(
        [
            part.reshape(kx_count // STACK, 2 * STACK, 2, extent)
            for part in (plain_rows, turned_rows)
        ],
        axis=1,
    ).reshape(4 * kx_count, 2, extent)
    mix_rows = jnp.asarray(split_rows(grouped, groups).astype(BF16))
    adjoint_rows = jnp.asarray(
        split_rows(np.concatenate([plain_rows, -turned_rows]), groups).astype(BF16)
    )
    back_rows = jnp.asarray(
        split_rows(plain_rows, groups).transpose(0, 2, 1).astype(BF16)
    )
    place = lax.axis_index("dp").astype(jnp.int32).reshape(1)

    exchange_shape = jax.ShapeDtypeStruct((groups, slots, lines), BF16)
    lines_shape = pltpu.HBM((lines, length), BF16)
    steps = length // TILE

    def exchange(values):
        return lax.all_to_all(values, "space", 0, 0, tiled=True)

    def mix(got, rows, given):
        adjoint = bool(given)
        shape = (mode_rows, 2 * kx_count // samples, LANES)
        block = jax.ShapeDtypeStruct((2,) + shape if adjoint else shape, BF16)
        outs = pl.pallas_call(
            lambda *refs: modes_kernel(*refs, adjoint=adjoint, samples=samples),
            out_shape=[exchange_shape] + [block] * samples,
            in_specs=[pl.BlockSpec(memory_space=pltpu.SMEM)] + [VMEM] * (4 + len(given)),
            out_specs=[VMEM] * (1 + samples),
            scratch_shapes=[
                pltpu.VMEM((lines // LANES, groups * slots, LANES), F32),
                pltpu.VMEM((rows_here * groups, mode_rows * LANES), BF16),
                pltpu.VMEM((mode_rows, 2 * kx_count, LANES), F32),
                pltpu.VMEM((2 * kx_count, mode_rows * LANES), F32),
            ],
            compiler_params=params(10),
            cost_estimate=cost(16),
            name="adjoint_modes" if adjoint else "mix_modes",
        )(place, got, mode_weight, rows, back_rows, *given)
        return outs[0], outs[1:]

    def share(blocks):
        return [blocks[0]] + [
            lax.ppermute(
                blocks[k], "dp", [(a, (a + k) % samples) for a in range(samples)]
            )
            for k in range(1, samples)
        ]

    columns, near_signal = pl.pallas_call(
        columns_kernel,
        out_shape=[exchange_shape, jax.ShapeDtypeStruct((lines, length), BF16)],
        in_specs=[HBM] * 4,
        out_specs=[VMEM, VMEM],
        scratch_shapes=[
            pltpu.VMEM(table.shape, BF16),
            pltpu.VMEM((2 * ky_count, lines), F32),
            pltpu.SemaphoreType.DMA((2, length // LOAD_TILE)),
        ],
        compiler_params=params(14),
        cost_estimate=cost(16),
        name="columns",
    )(pinned(table), pinned(signal), pinned(upstream), pinned(mode_weight))
    columns, place = lax.optimization_barrier((columns, place))
    sent, spectrum = mix(exchange(columns), mix_rows, ())
    back = exchange(sent)
    response, delta, delta_columns = pl.pallas_call(
        field_kernel,
        out_shape=[lines_shape, lines_shape, exchange_shape],
        in_specs=[VMEM] * 5,
        out_specs=[HBM, HBM, VMEM],
        scratch_shapes=[pltpu.VMEM((lines, length), BF16)] * 2
        + [
            pltpu.VMEM((lines, 2 * ky_count), BF16),
            pltpu.VMEM((DIAGONAL, DIAGONAL), BF16),
            pltpu.VMEM((2, lines, TILE), F32),
            pltpu.VMEM((2 * ky_count, lines), F32),
            pltpu.SemaphoreType.DMA((2, steps)),
        ],
        compiler_params=params(20),
        cost_estimate=cost(24),
        name="field_step",
    )(back, table, near_signal, upstream, mix_weight)
    sent, both_modes = mix(exchange(delta_columns), adjoint_rows, spectrum)
    shared = share(both_modes)
    back = exchange(sent)
    modes_shape = pltpu.HBM((mode_rows, kx_count // samples, channels, LANES), F32)
    field_grad, mode_grad = pl.pallas_call(
        lambda *refs: grad_kernel(*refs, samples=samples),
        out_shape=[lines_shape, modes_shape],
        in_specs=[VMEM, VMEM, HBM, VMEM] + [VMEM] * samples,
        out_specs=[HBM, HBM],
        scratch_shapes=[
            pltpu.VMEM((lines, length), BF16),
            pltpu.VMEM((lines, 2 * ky_count), BF16),
            pltpu.VMEM((DIAGONAL, DIAGONAL), BF16),
            pltpu.VMEM((lines, length), BF16),
            pltpu.VMEM(modes_shape.shape, F32),
            pltpu.SemaphoreType.DMA(
                (2 + lines // DIAGONAL, max(length // LOAD_TILE, mode_rows))
            ),
        ],
        compiler_params=params(20),
        cost_estimate=cost(16),
        name="gradients",
    )(back, table, pinned(delta), mix_weight, *shared)
    return (response.reshape(fields.shape), field_grad.reshape(fields.shape), mode_grad)


def solution(mesh):
    in_specs = (
        P("dp", "space", None, None),
        P("dp", "space", None, None),
        P("space", None, None, None),
        P(),
    )
    out_specs = (
        P("dp", "space", None, None),
        P("dp", "space", None, None),
        P("space", "dp", None, None),
    )
    return jax.shard_map(
        on_device, mesh=mesh, in_specs=in_specs, out_specs=out_specs, check_vma=False
    )
```

```python
import math

import jax
import jax.numpy as jnp
import numpy as np
from jax import lax
from jax.experimental import pallas as pl
from jax.experimental.pallas import tpu as pltpu
from jax.sharding import PartitionSpec as P

GELU_CUBIC = 0.044715
GELU_SCALE = math.sqrt(2.0 / math.pi)
LANES = 128
BF16 = jnp.bfloat16
F32 = jnp.float32
STACK = 4
TILE = 512
DIAGONAL = 256
LOAD_TILE = 1024
AHEAD = 4
MIB = 1024 * 1024


def trig(phase_index, extent):
    angles = phase_index.astype(np.float32) * np.float32(2.0 * math.pi / extent)
    norm_scale = np.float32(1.0 / math.sqrt(extent))
    return (
        (np.cos(angles) * norm_scale).astype(BF16).astype(np.float32),
        (np.sin(angles) * norm_scale).astype(BF16).astype(np.float32),
    )


def column_table(length, mode_count, owners):
    phase = np.arange(mode_count)[:, None] * np.arange(length)[None, :] % length
    cos_part, sin_part = trig(phase, length)
    both = np.stack([cos_part, -sin_part]).reshape(2, owners, mode_count // owners, length)
    return both.transpose(1, 0, 2, 3).reshape(2 * mode_count, length).astype(BF16)


def row_matrix(extent, mode_count):
    slot = np.arange(mode_count)
    frequency = np.where(slot < mode_count // 2, slot, extent - mode_count + slot)
    phase = frequency[:, None] * np.arange(extent)[None, :] % extent
    cos_part, sin_part = trig(phase, extent)
    return np.stack(
        [np.stack([cos_part, sin_part], 1), np.stack([-sin_part, cos_part], 1)], 1
    )


def split_rows(matrix, owners):
    rows, parts, extent = matrix.shape
    split = matrix.reshape(rows, parts, owners, extent // owners // 2, 2)
    split = split.transpose(4, 0, 1, 3, 2)
    return split.reshape(2, rows, parts * extent // 2)


def half_mask(shape):
    return lax.broadcasted_iota(jnp.int32, shape, len(shape) - 1) % LANES < LANES // 2


def fold(first, second):
    picked = jnp.where(half_mask(first.shape), first, second)
    return picked + pltpu.roll(picked, LANES // 2, 1)


def dot_nt(left, right):
    return lax.dot_general(left, right, (((1,), (1,)), ((), ())), preferred_element_type=F32)


def dot_nn(left, right):
    return jnp.dot(left, right, preferred_element_type=F32)


def weigh(values, mode_rows):
    row = lax.broadcasted_iota(jnp.int32, values.shape, 0)
    return jnp.where((row == 0) | (row == mode_rows), values, values * 2.0)


def tiles(length, size):
    return [slice(at, at + size) for at in range(0, length, size)]


class Loads:
    def __init__(self, pairs, sem_ref, size):
        self.copies = [
            [
                pltpu.make_async_copy(source.at[:, cols], target.at[:, cols], sem_ref.at[n, k])
                for n, (source, target) in enumerate(pairs)
            ]
            for k, cols in enumerate(tiles(pairs[0][0].shape[1], size))
        ]
        for k in range(AHEAD):
            self.start(k)

    def start(self, k):
        if k < len(self.copies):
            for copy in self.copies[k]:
                copy.start()

    def wait(self, k):
        for copy in self.copies[k]:
            copy.wait()
        self.start(k + AHEAD)


def columns_kernel(
    table_hbm, fields_hbm, upstream_hbm, weight_hbm,
    out_ref, fields_ref, table_ref, acc_ref, sem_ref,
):
    del upstream_hbm, weight_hbm
    parts = tiles(table_hbm.shape[1], LOAD_TILE)
    loads = Loads(((table_hbm, table_ref), (fields_hbm, fields_ref)), sem_ref, LOAD_TILE)
    for k, cols in enumerate(parts):
        loads.wait(k)
        product = dot_nt(table_ref[:, cols], fields_ref[:, cols])
        if k == 0:
            acc_ref[...] = product
        elif k < len(parts) - 1:
            acc_ref[...] += product
        else:
            out_ref[...] = (acc_ref[...] + product).reshape(out_ref.shape).astype(BF16)


def gather_rows(got_ref, flat_ref, z_ref):
    owners, slots, width = got_ref.shape
    mode_rows = slots // 2
    for h in range(width // LANES):
        part = got_ref[:, :, h * LANES : (h + 1) * LANES].astype(F32)
        flat_ref[h] = part.reshape(owners * slots, LANES)
    for p in range(2):
        for i in range(mode_rows):
            for h in range(width // LANES):
                block = flat_ref[h, pl.ds(p * mode_rows + i, owners, stride=slots), :]
                at = (p * (width // LANES) + h) * owners
                z_ref[at : at + owners, i * LANES : (i + 1) * LANES] = block.astype(BF16)


def scatter_rows(values, flat_ref, i, owners, slots):
    mode_rows = slots // 2
    columns = flat_ref.shape[0]
    for p in range(2):
        for h in range(columns):
            at = (p * columns + h) * owners
            flat_ref[h, pl.ds(p * mode_rows + i, owners, stride=slots), :] = values[
                at : at + owners
            ]


def modes_kernel(
    place_ref, got_ref, weight_ref, rows_ref, back_ref, *rest, adjoint, samples
):
    given = samples if adjoint else 0
    x_refs, sent_ref, shared_refs = rest[:given], rest[given], rest[given + 1 : given + 1 + samples]
    flat_ref, z_ref, mode_ref, y_ref = rest[given + 1 + samples :]
    owners, slots, _ = got_ref.shape
    mode_rows, kx_count, channels, _ = weight_ref.shape
    gather_rows(got_ref, flat_ref, z_ref)
    count = 2 * kx_count
    stack_rows = 2 * STACK
    first = dot_nn(rows_ref[0], z_ref[...])
    second = dot_nn(rows_ref[1], z_ref[...])
    for i in range(mode_rows):
        lanes = slice(i * LANES, (i + 1) * LANES)
        both = fold(first[:, lanes], second[:, lanes])
        if adjoint:
            plain, turned = both[:count], both[count:]
            left = jnp.where(half_mask(plain.shape), plain, turned)
            mode_ref[i] = left
            left = left.astype(BF16)
            row = lax.broadcasted_iota(jnp.int32, (stack_rows, LANES), 0) // 2
            low = half_mask((stack_rows, LANES))
            for g in range(kx_count // STACK):
                pair = left[g // 2 * 2 * stack_rows : (g // 2 + 1) * 2 * stack_rows]
                w = weight_ref[i, g * STACK : (g + 1) * STACK].reshape(STACK * channels, LANES)
                full = dot_nt(pair, w)[g % 2 * stack_rows : (g % 2 + 1) * stack_rows]
                picked = jnp.where(row < 2, full[:, :LANES], full[:, LANES:])
                picked = jnp.where((row % 2 == 0) == low, picked, 0.0)
                y_ref[g * stack_rows : (g + 1) * stack_rows, lanes] = picked + pltpu.roll(
                    picked, LANES // 2, 1
                )
        else:
            wide = jnp.concatenate([both, both], axis=1)
            lane = lax.broadcasted_iota(jnp.int32, wide.shape, 1) // channels
            row = lax.broadcasted_iota(jnp.int32, wide.shape, 0) % stack_rows // 2
            left = jnp.where(lane == row, wide, 0.0).astype(BF16)
            for g in range(kx_count // STACK):
                rows = slice(g * 2 * stack_rows, (g + 1) * 2 * stack_rows)
                mode_ref[i, g * stack_rows : (g + 1) * stack_rows, :] = both[rows][:stack_rows]
                w = weight_ref[i, g * STACK : (g + 1) * STACK].reshape(STACK * channels, LANES)
                full = dot_nn(left[rows], w)
                y_ref[g * stack_rows : (g + 1) * stack_rows, lanes] = fold(
                    full[:stack_rows], full[stack_rows:]
                )
    y = y_ref[...].astype(BF16)
    first, second = dot_nn(back_ref[0], y), dot_nn(back_ref[1], y)
    values = jnp.where(half_mask(first.shape), first, second)
    for i in range(mode_rows):
        scatter_rows(values[:, i * LANES : (i + 1) * LANES], flat_ref, i, owners, slots)
    for h in range(flat_ref.shape[0]):
        part = flat_ref[h].reshape(owners, slots, LANES)
        sent_ref[:, :, h * LANES : (h + 1) * LANES] = part.astype(BF16)
    block = count // samples
    for k, shared_ref in enumerate(shared_refs):
        start = pl.multiple_of((place_ref[0] + k) % samples * block, block)
        if adjoint:
            shared_ref[0] = x_refs[k][...]
        for i in range(mode_rows):
            values = mode_ref[i, pl.ds(start, block), :].astype(BF16)
            if adjoint:
                shared_ref[1, i] = values
            else:
                shared_ref[i] = values


def transpose_back(back_ref, turned_ref, mode_rows, weighted):
    owners, slots, width = back_ref.shape
    for at in range(0, width, DIAGONAL):
        flat = back_ref[:, :, at : at + DIAGONAL].astype(F32).reshape(owners * slots, DIAGONAL)
        if weighted:
            flat = weigh(flat, mode_rows)
        turned_ref[at : at + DIAGONAL, :] = flat.T.astype(BF16)


def spread(block, out_ref):
    out_ref[...] = jnp.zeros_like(out_ref)
    size = block.shape[0]
    for at in range(0, out_ref.shape[0], size):
        out_ref[at : at + size, at : at + size] = block


def gelu_chunk(pre_ref, upstream_ref, response_ref, delta_ref, slot, rows, cols):
    v = pre_ref[slot, rows, :]
    t = jnp.tanh(v * (GELU_SCALE + (GELU_SCALE * GELU_CUBIC) * (v * v)))
    scaled = 0.5 * t
    half = (0.5 + scaled).astype(BF16)
    other = (0.5 - scaled).astype(BF16)
    v = v.astype(BF16)
    value = v * half
    response_ref[rows, cols] = value
    inner = (2.0 * GELU_SCALE) + (6.0 * GELU_SCALE * GELU_CUBIC) * (v * v)
    delta_ref[rows, cols] = upstream_ref[rows, cols] * (half + value * other * inner)


def field_kernel(
    back_ref, table_ref, fields_ref, upstream_ref, weight_ref,
    response_hbm, delta_hbm, sent_ref,
    response_ref, delta_ref, turned_ref, mix_ref, pre_ref, acc_ref, sem_ref,
):
    mode_rows = back_ref.shape[1] // 2
    spread(weight_ref[...].astype(F32).T.astype(BF16), mix_ref)
    transpose_back(back_ref, turned_ref, mode_rows, True)
    width = mix_ref.shape[0]
    total = fields_ref.shape[0]
    chunk = 32
    parts = tiles(table_ref.shape[1], TILE)
    copies = []

    def preact(k, at):
        rows = slice(at, at + width)
        pre_ref[k % 2, rows, :] = dot_nn(turned_ref[rows, :], table_ref[:, parts[k]]) + dot_nn(
            mix_ref[...], fields_ref[rows, parts[k]]
        )

    for at in range(0, total, width):
        preact(0, at)
    for k, cols in enumerate(parts):
        for at in range(0, total, chunk):
            if at % width == 0 and k + 1 < len(parts):
                preact(k + 1, at)
            rows = slice(at, at + chunk)
            gelu_chunk(pre_ref, upstream_ref, response_ref, delta_ref, k % 2, rows, cols)
        for n, (source, target) in enumerate(
            ((response_ref, response_hbm), (delta_ref, delta_hbm))
        ):
            copies.append(
                pltpu.make_async_copy(
                    source.at[:, cols], target.at[:, cols], sem_ref.at[n, k]
                )
            )
            copies[-1].start()
        product = dot_nt(table_ref[:, cols], delta_ref[:, cols])
        if k == 0:
            acc_ref[...] = product
        elif k < len(parts) - 1:
            acc_ref[...] += product
        else:
            sent = weigh(acc_ref[...] + product, mode_rows)
            sent_ref[...] = sent.reshape(sent_ref.shape).astype(BF16)
    for copy in copies:
        copy.wait()


def mode_products(shared_refs, out_ref, i):
    _, kx_here, channels, _ = out_ref.shape
    stack_rows = 2 * STACK
    count = len(shared_refs) * stack_rows
    row = lax.broadcasted_iota(jnp.int32, (count, LANES), 0) % stack_rows // 2
    for g in range(kx_here // STACK):
        rows = slice(g * stack_rows, (g + 1) * stack_rows)
        x = jnp.concatenate([ref[0, i, rows, :].astype(F32) for ref in shared_refs], axis=0)
        d = jnp.concatenate([ref[1, i, rows, :].astype(F32) for ref in shared_refs], axis=0)
        wide = jnp.concatenate([jnp.where(row == m, d, 0.0) for m in range(STACK)], axis=1)
        product = dot_nn(x.T[:channels].astype(BF16), wide.astype(BF16))
        for m in range(STACK):
            out_ref[i, g * STACK + m] = product[:, m * LANES : (m + 1) * LANES]


def grad_kernel(back_ref, table_ref, delta_hbm, weight_ref, *rest, samples):
    shared_refs, (out_hbm, modes_hbm) = rest[:samples], rest[samples : samples + 2]
    delta_ref, turned_ref, mix_ref, out_ref, modes_ref, sem_ref = rest[samples + 2 :]
    loads = Loads(((delta_hbm, delta_ref),), sem_ref, LOAD_TILE)
    spread(weight_ref[...], mix_ref)
    transpose_back(back_ref, turned_ref, 0, False)
    width = mix_ref.shape[0]
    copies = []

    def modes(first, last):
        for i in range(first, last):
            mode_products(shared_refs, modes_ref, i)
            copies.append(pltpu.make_async_copy(modes_ref.at[i], modes_hbm.at[i], sem_ref.at[1, i]))
            copies[-1].start()

    mode_rows = modes_ref.shape[0]
    modes(0, mode_rows // 2)
    for k, cols in enumerate(tiles(table_ref.shape[1], LOAD_TILE)):
        loads.wait(k)
        for n, at in enumerate(range(0, delta_ref.shape[0], width)):
            rows = slice(at, at + width)
            out_ref[rows, cols] = (
                dot_nn(turned_ref[rows, :], table_ref[:, cols])
                + dot_nn(mix_ref[...], delta_ref[rows, cols])
            ).astype(BF16)
            copies.append(
                pltpu.make_async_copy(
                    out_ref.at[rows, cols], out_hbm.at[rows, cols], sem_ref.at[2 + n, k]
                )
            )
            copies[-1].start()
    modes(mode_rows // 2, mode_rows)
    for copy in copies:
        copy.wait()


VMEM = pl.BlockSpec(memory_space=pltpu.VMEM)
HBM = pl.BlockSpec(memory_space=pltpu.HBM)


def pinned(values):
    return pltpu.with_memory_space_constraint(values, pltpu.HBM)


def cost(mib):
    return pl.CostEstimate(flops=0, transcendentals=0, bytes_accessed=mib * MIB)


def params(mib):
    return pltpu.CompilerParams(vmem_limit_bytes=mib * MIB)


def on_device(fields, cotangent, mode_weight, mix_weight):
    _, rows_here, channels, length = fields.shape
    mode_rows, kx_count = mode_weight.shape[:2]
    groups = lax.axis_size("space")
    samples = lax.axis_size("dp")
    ky_count = mode_rows * groups
    extent = rows_here * groups
    lines = rows_here * channels
    slots = 2 * mode_rows
    signal = fields.reshape(lines, length)
    upstream = cotangent.reshape(lines, length)
    table = jnp.asarray(column_table(length, ky_count, groups))
    matrix = row_matrix(extent, kx_count)
    turned = np.stack([-matrix[:, 1], matrix[:, 0]], 1)
    plain_rows = matrix.reshape(2 * kx_count, 2, extent)
    turned_rows = turned.reshape(2 * kx_count, 2, extent)
    grouped = np.concatenate(
        [
            part.reshape(kx_count // STACK, 2 * STACK, 2, extent)
            for part in (plain_rows, turned_rows)
        ],
        axis=1,
    ).reshape(4 * kx_count, 2, extent)
    mix_rows = jnp.asarray(split_rows(grouped, groups).astype(BF16))
    adjoint_rows = jnp.asarray(
        split_rows(np.concatenate([plain_rows, -turned_rows]), groups).astype(BF16)
    )
    back_rows = jnp.asarray(
        split_rows(plain_rows, groups).transpose(0, 2, 1).astype(BF16)
    )
    place = lax.axis_index("dp").astype(jnp.int32).reshape(1)

    exchange_shape = jax.ShapeDtypeStruct((groups, slots, lines), BF16)
    lines_shape = pltpu.HBM((lines, length), BF16)
    steps = length // TILE

    def exchange(values):
        return lax.all_to_all(values, "space", 0, 0, tiled=True)

    def mix(got, rows, given):
        adjoint = bool(given)
        shape = (mode_rows, 2 * kx_count // samples, LANES)
        block = jax.ShapeDtypeStruct((2,) + shape if adjoint else shape, BF16)
        outs = pl.pallas_call(
            lambda *refs: modes_kernel(*refs, adjoint=adjoint, samples=samples),
            out_shape=[exchange_shape] + [block] * samples,
            in_specs=[pl.BlockSpec(memory_space=pltpu.SMEM)] + [VMEM] * (4 + len(given)),
            out_specs=[VMEM] * (1 + samples),
            scratch_shapes=[
                pltpu.VMEM((lines // LANES, groups * slots, LANES), F32),
                pltpu.VMEM((rows_here * groups, mode_rows * LANES), BF16),
                pltpu.VMEM((mode_rows, 2 * kx_count, LANES), F32),
                pltpu.VMEM((2 * kx_count, mode_rows * LANES), F32),
            ],
            compiler_params=params(10),
            cost_estimate=cost(16),
            name="adjoint_modes" if adjoint else "mix_modes",
        )(place, got, mode_weight, rows, back_rows, *given)
        return outs[0], outs[1:]

    def share(blocks):
        return [blocks[0]] + [
            lax.ppermute(
                blocks[k], "dp", [(a, (a + k) % samples) for a in range(samples)]
            )
            for k in range(1, samples)
        ]

    columns, near_signal = pl.pallas_call(
        columns_kernel,
        out_shape=[exchange_shape, jax.ShapeDtypeStruct((lines, length), BF16)],
        in_specs=[HBM] * 4,
        out_specs=[VMEM, VMEM],
        scratch_shapes=[
            pltpu.VMEM(table.shape, BF16),
            pltpu.VMEM((2 * ky_count, lines), F32),
            pltpu.SemaphoreType.DMA((2, length // LOAD_TILE)),
        ],
        compiler_params=params(14),
        cost_estimate=cost(16),
        name="columns",
    )(pinned(table), pinned(signal), pinned(upstream), pinned(mode_weight))
    columns, place = lax.optimization_barrier((columns, place))
    sent, spectrum = mix(exchange(columns), mix_rows, ())
    back = exchange(sent)
    response, delta, delta_columns = pl.pallas_call(
        field_kernel,
        out_shape=[lines_shape, lines_shape, exchange_shape],
        in_specs=[VMEM] * 5,
        out_specs=[HBM, HBM, VMEM],
        scratch_shapes=[pltpu.VMEM((lines, length), BF16)] * 2
        + [
            pltpu.VMEM((lines, 2 * ky_count), BF16),
            pltpu.VMEM((DIAGONAL, DIAGONAL), BF16),
            pltpu.VMEM((2, lines, TILE), F32),
            pltpu.VMEM((2 * ky_count, lines), F32),
            pltpu.SemaphoreType.DMA((2, steps)),
        ],
        compiler_params=params(20),
        cost_estimate=cost(24),
        name="field_step",
    )(back, table, near_signal, upstream, mix_weight)
    sent, both_modes = mix(exchange(delta_columns), adjoint_rows, spectrum)
    shared = share(both_modes)
    back = exchange(sent)
    modes_shape = pltpu.HBM((mode_rows, kx_count // samples, channels, LANES), F32)
    field_grad, mode_grad = pl.pallas_call(
        lambda *refs: grad_kernel(*refs, samples=samples),
        out_shape=[lines_shape, modes_shape],
        in_specs=[VMEM, VMEM, HBM, VMEM] + [VMEM] * samples,
        out_specs=[HBM, HBM],
        scratch_shapes=[
            pltpu.VMEM((lines, length), BF16),
            pltpu.VMEM((lines, 2 * ky_count), BF16),
            pltpu.VMEM((DIAGONAL, DIAGONAL), BF16),
            pltpu.VMEM((lines, length), BF16),
            pltpu.VMEM(modes_shape.shape, F32),
            pltpu.SemaphoreType.DMA(
                (2 + lines // DIAGONAL, max(length // LOAD_TILE, mode_rows))
            ),
        ],
        compiler_params=params(20),
        cost_estimate=cost(16),
        name="gradients",
    )(back, table, pinned(delta), mix_weight, *shared)
    return (response.reshape(fields.shape), field_grad.reshape(fields.shape), mode_grad)


def solution(mesh):
    in_specs = (
        P("dp", "space", None, None),
        P("dp", "space", None, None),
        P("space", None, None, None),
        P(),
    )
    out_specs = (
        P("dp", "space", None, None),
        P("dp", "space", None, None),
        P("space", "dp", None, None),
    )
    return jax.shard_map(
        on_device, mesh=mesh, in_specs=in_specs, out_specs=out_specs, check_vma=False
    )
```
